32 devices in a mesh: dom: 8 (over z, y), rep: 4 (over x, core).
Axes of the slice: x: 2, y: 2, z: 4, core: 2. Of those that a mesh axis runs over, the one named last changes fastest.
Arguments:
- node_features: bfloat16 [32768, 128], P(('rep', 'dom')), parts along dimension 0, may hold values from -6 to 6
- edge_features: bfloat16 [86016, 128], P(('rep', 'dom')), parts along dimension 0, may hold values from -6 to 6
- node_cotangent: bfloat16 [32768, 128], P(('rep', 'dom')), parts along dimension 0, may hold values from -6 to 6
- edge_cotangent: bfloat16 [86016, 128], P(('rep', 'dom')), parts along dimension 0, may hold values from -6 to 6
- edge_in_weight: bfloat16 [384, 128], replicated, may hold values from -0.3125 to 0.3125
- edge_in_bias: float32 [128], replicated, may hold values from -3 to 3
- edge_out_weight: bfloat16 [128, 128], replicated, may hold values from -0.5 to 0.5
- edge_out_bias: float32 [128], replicated, may hold values from -3 to 3
- node_in_weight: bfloat16 [256, 128], replicated, may hold values from -0.375 to 0.375
- node_in_bias: float32 [128], replicated, may hold values from -3 to 3
- node_out_weight: bfloat16 [128, 128], replicated, may hold values from -0.5 to 0.5
- edge_ends: int32 [2, 1344], replicated, may hold values from 0 to 511, as said below
- live_elements: int32 [32], P(('rep', 'dom')), parts along dimension 0, may hold values from 1 to 2, as said below
- shared_nodes: int32 [32, 4, 128], P(('rep', 'dom')), parts along dimension 0, may hold values from 0 to 1023, as said below
- shared_counts: int32 [32, 4], P(('rep', 'dom')), parts along dimension 0, may hold values from 32 to 128, as said below
- multiplicity: int32 [32768], P(('rep', 'dom')), parts along dimension 0, may hold values from 1 to 515
Outputs:
- node_gradient: bfloat16 [32768, 128], P(('rep', 'dom')), parts along dimension 0
- edge_gradient: bfloat16 [86016, 128], P(('rep', 'dom')), parts along dimension 0
- edge_in_weight_gradient: float32 [1536, 128], P('rep'), parts along dimension 0
- edge_in_bias_gradient: float32 [512], P('rep'), parts along dimension 0
- edge_out_weight_gradient: float32 [512, 128], P('rep'), parts along dimension 0
- edge_out_bias_gradient: float32 [512], P('rep'), parts along dimension 0
- node_in_weight_gradient: float32 [1024, 128], P('rep'), parts along dimension 0
- node_in_bias_gradient: float32 [512], P('rep'), parts along dimension 0
- node_out_weight_gradient: float32 [512, 128], P('rep'), parts along dimension 0
- node_out_bias_gradient: float32 [512], P('rep'), parts along dimension 0
The draws below stay inside these ranges and needn't reach their ends.
There are 4 independent parts, one for each index of `rep`. The reference program is written for one: setup_inputs(seed, part) draws one part's arguments, and reference() takes and returns one part's arrays. A program takes and returns all parts, laid end to end along the dimension named above; an argument that names none is the same for every part. Nothing has to cross between parts.
Inputs may be any that keep to these rules, and one draw needn't show every extreme that they name: `edge_ends`: each edge joins two nodes next to each other on the element's 8 x 8 x 8 lattice of nodes. `live_elements`: some partition has all 2 slots live. `shared_nodes`: entry s of a partition's list for neighbour k is the node paired with entry s of that neighbour's list for neighbour k xor 1; entries below the count name nodes of live slots; entries at or beyond it are 0. `shared_counts`: both lists of a pair have the same count; some pair has 128 entries.
All inputs are finite; a program needn't handle non-finite values.
Results may differ from the reference program's by a relative error of at most 0.0056.
Values sent between devices are 32-bit elements; how exact they have to be, the bound alone decides.
A program may use at most 64 MiB of HBM per device.

```python
import math
import jax
import jax.numpy as jnp
from jax import lax

D = 128
HID = 128
NPE = 512
EPE = 1344
S_MAX = 128
E_DEV = 2
NODES = 8192
EDGES = 21504
N_DOM = 8


def draw_layout(key):
    subkeys = [jax.random.fold_in(key, 7001 + number) for number in range(8)]
    device = jnp.arange(N_DOM, dtype=jnp.int32)
    raw_draw = jax.random.randint(subkeys[0], (N_DOM,), 0, E_DEV + 1, dtype=jnp.int32)
    element_counts = jnp.minimum(1 + raw_draw * raw_draw // E_DEV, E_DEV)
    busiest = jax.random.randint(subkeys[1], (), 0, N_DOM, dtype=jnp.int32)
    element_counts = jnp.where(device == busiest, E_DEV, element_counts).astype(jnp.int32)
    quarter = N_DOM // 4
    pair_lengths = jax.random.randint(subkeys[2], (2 * N_DOM,), max(S_MAX // 4, 1), S_MAX + 1, dtype=jnp.int32)
    full_pair = jax.random.randint(subkeys[3], (), 0, 2 * N_DOM, dtype=jnp.int32)
    pair_lengths = jnp.where(jnp.arange(2 * N_DOM, dtype=jnp.int32) == full_pair, S_MAX, pair_lengths).reshape(2, N_DOM)
    hop_sizes = jnp.array([1, quarter], dtype=jnp.int32)
    upper_device = (device[None, :] + hop_sizes[:, None]) % N_DOM
    lower_device = (device[None, :] - hop_sizes[:, None]) % N_DOM
    entry_index = jnp.arange(S_MAX, dtype=jnp.int32)[None, None, :]
    low_side = jax.random.randint(subkeys[4], (2, N_DOM, S_MAX), 0, element_counts[None, :, None] * NPE, dtype=jnp.int32)
    high_side = jax.random.randint(subkeys[5], (2, N_DOM, S_MAX), 0, element_counts[upper_device][:, :, None] * NPE, dtype=jnp.int32)
    entry_used = entry_index < pair_lengths[:, :, None]
    low_side = jnp.where(entry_used, low_side, 0)
    high_side = jnp.where(entry_used, high_side, 0)
    kinds = jnp.arange(2, dtype=jnp.int32)[:, None]
    from_high = high_side[kinds, lower_device]
    node_lists = jnp.stack([low_side[0], from_high[0], low_side[1], from_high[1]], axis=1).astype(jnp.int32)
    high_lengths = pair_lengths[kinds, lower_device]
    list_lengths = jnp.stack([pair_lengths[0], high_lengths[0], pair_lengths[1], high_lengths[1]], axis=1).astype(jnp.int32)
    listed = (entry_index < list_lengths[:, :, None]).astype(jnp.int32).reshape(-1)
    rows = (device[:, None, None] * (E_DEV * NPE) + node_lists).reshape(-1)
    appearances = jnp.zeros((N_DOM * E_DEV * NPE,), jnp.int32).at[rows].add(listed)
    extra_copies = jax.random.randint(subkeys[6], (N_DOM * E_DEV * NPE,), 0, 3, dtype=jnp.int32)
    copies = jnp.minimum(1 + appearances + extra_copies, 4 * S_MAX + 3)
    crowded = jax.random.randint(subkeys[7], (), 0, N_DOM * E_DEV * NPE, dtype=jnp.int32)
    copies = jnp.where(jnp.arange(N_DOM * E_DEV * NPE, dtype=jnp.int32) == crowded, 4 * S_MAX + 3, copies).astype(jnp.int32)
    return (element_counts, node_lists, list_lengths, copies)


def draw_live_elements(key, part):
    return draw_layout(key)[0]


def draw_shared_nodes(key, part):
    return draw_layout(key)[1]


def draw_shared_counts(key, part):
    return draw_layout(key)[2]


def draw_multiplicity(key, part):
    return draw_layout(key)[3]


def draw_edge_ends(key, part):
    start_node = jax.random.randint(jax.random.fold_in(key, 9101), (EPE,), 0, NPE, dtype=jnp.int32)
    direction = jax.random.randint(jax.random.fold_in(key, 9102), (EPE,), 0, 3, dtype=jnp.int32)
    step_sign = 2 * jax.random.randint(jax.random.fold_in(key, 9103), (EPE,), 0, 2, dtype=jnp.int32) - 1
    stride = jnp.where(direction == 0, 64, jnp.where(direction == 1, 8, 1)).astype(jnp.int32)
    coordinate = start_node // stride % 8
    outside = (coordinate + step_sign < 0) | (coordinate + step_sign > 7)
    step_sign = jnp.where(outside, -step_sign, step_sign)
    return jnp.stack([start_node, start_node + step_sign * stride]).astype(jnp.int32)


def steps_of(stream_key, dims, split, low, top_value):
    def one(dim, parts):
        draws = jax.random.uniform(jax.random.fold_in(jax.random.fold_in(stream_key, 6), dim), (parts,), jnp.float32, low / len(split), top_value / len(split))
        return jnp.repeat(jnp.exp(draws), dims[dim] // parts).reshape((-1,) + (1,) * (len(dims) - dim - 1))

    factor_of = one(*split[0])
    for cut in split[1:]:
        factor_of = factor_of * one(*cut)
    return factor_of


def bell_draw(rng, extent, width, reach, pieces=(), held_as=jnp.bfloat16):
    entries = width * jax.random.normal(rng, extent, jnp.float32)
    if pieces:
        entries = entries * steps_of(rng, extent, pieces, -0.22, 0.18)
    return jnp.clip(entries, -reach, reach).astype(held_as)


def setup_inputs(seed: int = 0, part: int = 0) -> dict:
    key_list = jax.random.split(jax.random.key(seed), 17)
    part_splits = jax.random.split(jax.random.fold_in(key_list[16], part), 17)
    return {
        "node_features": bell_draw(part_splits[0], (NODES, D), 1.0, 6.0, ((0, 8),)),
        "edge_features": bell_draw(part_splits[1], (EDGES, D), 1.0, 6.0, ((0, 8),)),
        "node_cotangent": bell_draw(part_splits[2], (NODES, D), 1.0, 6.0, ((0, 8),)),
        "edge_cotangent": bell_draw(part_splits[3], (EDGES, D), 1.0, 6.0, ((0, 8),)),
        "edge_in_weight": bell_draw(key_list[4], (3 * D, HID), (3 * D) ** -0.5, 0.3125),
        "edge_in_bias": bell_draw(key_list[5], (HID,), 0.5, 3.0, (), jnp.float32),
        "edge_out_weight": bell_draw(key_list[6], (HID, D), HID ** -0.5, 0.5),
        "edge_out_bias": bell_draw(key_list[7], (D,), 0.5, 3.0, (), jnp.float32),
        "node_in_weight": bell_draw(key_list[8], (2 * D, HID), (2 * D) ** -0.5, 0.375),
        "node_in_bias": bell_draw(key_list[9], (HID,), 0.5, 3.0, (), jnp.float32),
        "node_out_weight": bell_draw(key_list[10], (HID, D), HID ** -0.5, 0.5),
        "edge_ends": draw_edge_ends(jax.random.fold_in(key_list[16], 71), part),
        "live_elements": draw_live_elements(jax.random.fold_in(jax.random.fold_in(key_list[16], part), 71), part),
        "shared_nodes": draw_shared_nodes(jax.random.fold_in(jax.random.fold_in(key_list[16], part), 71), part),
        "shared_counts": draw_shared_counts(jax.random.fold_in(jax.random.fold_in(key_list[16], part), 71), part),
        "multiplicity": draw_multiplicity(jax.random.fold_in(jax.random.fold_in(key_list[16], part), 71), part),
    }


def silu_slope(linear):
    squashed = jax.nn.sigmoid(linear)
    return squashed * (1.0 + linear * (1.0 - squashed))

def contract_rows(left, right):
    return lax.dot_general(left, right, (((0,), (0,)), ((), ())), preferred_element_type=jnp.float32)

def edge_forward(blocks, edge_rows, edge_ends, edge_in_weight, edge_in_bias, edge_out_weight, edge_out_bias):
    feature_width = blocks.shape[2]
    source = jnp.take(blocks, edge_ends[0], axis=1).reshape(-1, feature_width)
    target = jnp.take(blocks, edge_ends[1], axis=1).reshape(-1, feature_width)
    joined = jnp.concatenate([source, target, edge_rows], axis=1)
    edge_linear = jnp.dot(joined, edge_in_weight, preferred_element_type=jnp.float32) + edge_in_bias
    edge_hidden = jax.nn.silu(edge_linear).astype(jnp.bfloat16)
    new_edges = edge_rows.astype(jnp.float32) + jnp.dot(edge_hidden, edge_out_weight, preferred_element_type=jnp.float32) + edge_out_bias
    return (joined, edge_linear, edge_hidden, new_edges)

def collect(new_edges, edge_ends, slot_count, element_nodes):
    feature_width = new_edges.shape[1]
    grouped = new_edges.reshape(slot_count, -1, feature_width)
    return jnp.zeros((slot_count, element_nodes, feature_width), jnp.float32).at[:, edge_ends[1]].add(grouped)

def edge_backward(joined, edge_linear, edge_hidden, edge_cot, edge_ends, edge_in_weight, edge_out_weight, slot_count, element_nodes):
    feature_width = edge_cot.shape[1]
    cot_half = edge_cot.astype(jnp.bfloat16)
    out_weight_term = contract_rows(edge_hidden, cot_half)
    out_bias_term = lax.optimization_barrier(jnp.sum(cot_half.astype(jnp.float32), axis=0))
    hidden_back = jnp.dot(cot_half, edge_out_weight.T, preferred_element_type=jnp.float32)
    edge_back = (hidden_back * silu_slope(edge_linear)).astype(jnp.bfloat16)
    in_weight_term = contract_rows(joined, edge_back)
    in_bias_term = lax.optimization_barrier(jnp.sum(edge_back.astype(jnp.float32), axis=0))
    joined_back = jnp.dot(edge_back, edge_in_weight.T, preferred_element_type=jnp.float32)
    from_source = joined_back[:, :feature_width].reshape(slot_count, -1, feature_width)
    from_target = joined_back[:, feature_width:2 * feature_width].reshape(slot_count, -1, feature_width)
    block_back = jnp.zeros((slot_count, element_nodes, feature_width), jnp.float32)
    block_back = block_back.at[:, edge_ends[0]].add(from_source).at[:, edge_ends[1]].add(from_target)
    edge_result = (edge_cot + joined_back[:, 2 * feature_width:]).astype(jnp.bfloat16)
    return (block_back, edge_result, (in_weight_term, in_bias_term, out_weight_term, out_bias_term))

def reference(node_features, edge_features, node_cotangent, edge_cotangent, edge_in_weight, edge_in_bias, edge_out_weight, edge_out_bias, node_in_weight, node_in_bias, node_out_weight, edge_ends, live_elements, shared_nodes, shared_counts, multiplicity):
    device_nodes = E_DEV * NPE
    device_edges = E_DEV * EPE
    live_slots = jnp.arange(E_DEV, dtype=jnp.int32)[None, :] < live_elements[:, None]
    node_live = jnp.repeat(live_slots, NPE, axis=1).reshape(-1)
    edge_live = jnp.repeat(live_slots, EPE, axis=1).reshape(-1)
    node_cot = jnp.where(node_live[:, None], node_cotangent, jnp.zeros_like(node_cotangent))
    edge_given = jnp.where(edge_live[:, None], edge_cotangent.astype(jnp.float32), jnp.zeros((1, D), jnp.float32))
    node_blocks = node_features.reshape(N_DOM, E_DEV, NPE, D)
    edge_blocks = edge_features.reshape(N_DOM, device_edges, D)

    def forward_device(bundle):
        outputs = edge_forward(bundle[0], bundle[1], edge_ends, edge_in_weight, edge_in_bias, edge_out_weight, edge_out_bias)
        return collect(outputs[3], edge_ends, E_DEV, NPE)
    aggregate = lax.map(forward_device, (node_blocks, edge_blocks)).reshape(NODES, D)
    quarter = N_DOM // 4
    offsets = jnp.array([1, -1, quarter, -quarter], dtype=jnp.int32)
    device = jnp.arange(N_DOM, dtype=jnp.int32)[:, None, None]
    neighbour = jnp.arange(4, dtype=jnp.int32)[None, :, None]
    entry_index = jnp.arange(S_MAX, dtype=jnp.int32)[None, None, :]
    partner_device = (device + offsets[neighbour]) % N_DOM
    own_rows = (device * device_nodes + shared_nodes).reshape(-1).astype(jnp.int32)
    partner_rows = (partner_device * device_nodes + shared_nodes[partner_device, neighbour ^ 1, entry_index]).reshape(-1).astype(jnp.int32)
    entry_valid = (entry_index < shared_counts[:, :, None]).reshape(-1)

    def partner_sum(values):
        moved = jnp.where(entry_valid[:, None], values[partner_rows], jnp.zeros((1, D), jnp.float32))
        return values + jnp.zeros_like(values).at[own_rows].add(moved)
    copies = multiplicity[:, None].astype(jnp.float32)
    consistent = partner_sum(aggregate) / copies
    node_input = jnp.concatenate([node_features, consistent.astype(jnp.bfloat16)], axis=1)
    node_linear = jnp.dot(node_input, node_in_weight, preferred_element_type=jnp.float32) + node_in_bias
    node_hidden = jax.nn.silu(node_linear).astype(jnp.bfloat16)
    node_out_term = contract_rows(node_hidden, node_cot)
    node_out_bias_term = lax.optimization_barrier(jnp.sum(node_cot.astype(jnp.float32), axis=0))
    hidden_back = jnp.dot(node_cot, node_out_weight.T, preferred_element_type=jnp.float32)
    node_back = (hidden_back * silu_slope(node_linear)).astype(jnp.bfloat16)
    node_in_term = contract_rows(node_input, node_back)
    node_in_bias_term = lax.optimization_barrier(jnp.sum(node_back.astype(jnp.float32), axis=0))
    node_input_back = jnp.dot(node_back, node_in_weight.T, preferred_element_type=jnp.float32)
    consistent_back = node_input_back[:, D:] / copies
    aggregate_back = partner_sum(consistent_back)
    gathered_back = jnp.take(aggregate_back.reshape(N_DOM * E_DEV, NPE, D), edge_ends[1], axis=1).reshape(EDGES, D)
    edge_cot = edge_given + gathered_back

    def backward_device(bundle):
        joined, edge_linear, edge_hidden, unused = edge_forward(bundle[0], bundle[1], edge_ends, edge_in_weight, edge_in_bias, edge_out_weight, edge_out_bias)
        return edge_backward(joined, edge_linear, edge_hidden, bundle[2], edge_ends, edge_in_weight, edge_out_weight, E_DEV, NPE)
    block_back, edge_result, edge_terms = lax.map(backward_device, (node_blocks, edge_blocks, edge_cot.reshape(N_DOM, device_edges, D)))
    edge_scale = 1.0 / math.sqrt(EDGES)
    node_scale = 1.0 / math.sqrt(NODES)
    node_result = (node_cot.astype(jnp.float32) + node_input_back[:, :D] + block_back.reshape(NODES, D)).astype(jnp.bfloat16)
    return (node_result, edge_result.reshape(EDGES, D), lax.optimization_barrier(jnp.sum(edge_terms[0], axis=0)) * edge_scale, lax.optimization_barrier(jnp.sum(edge_terms[1], axis=0)) * edge_scale, lax.optimization_barrier(jnp.sum(edge_terms[2], axis=0)) * edge_scale, lax.optimization_barrier(jnp.sum(edge_terms[3], axis=0)) * edge_scale, node_in_term * node_scale, node_in_bias_term * node_scale, node_out_term * node_scale, node_out_bias_term * node_scale)
```

```python
import functools
import math

import jax
import jax.numpy as jnp
from jax import lax
from jax.experimental import pallas as pl
from jax.experimental.pallas import tpu as pltpu
from jax.sharding import PartitionSpec as P

NPE = 512
LANES = 128
F32 = jnp.float32
BF16 = jnp.bfloat16
MESH = pl.DeviceIdType.MESH


def divisor_up_to(total, cap):
    best = 16
    for size in range(16, cap + 1, 16):
        if total % size == 0:
            best = size
    return best


def mm(left, right):
    return lax.dot_general(left, right, (((1,), (0,)), ((), ())), preferred_element_type=F32)


def mm_rt(left, right):
    return lax.dot_general(left, right, (((1,), (1,)), ((), ())), preferred_element_type=F32)


def mm_lt(left, right):
    return lax.dot_general(left, right, (((0,), (0,)), ((), ())), preferred_element_type=F32)


def halves(value):
    high = value.astype(BF16)
    low = (value - high.astype(F32)).astype(BF16)
    return high, low


def columns_of(row):
    return jnp.transpose(jnp.broadcast_to(row, (LANES, row.shape[1])))


def hits(ids, width):
    lane = lax.broadcasted_iota(jnp.int32, ids.shape, 1).astype(F32)
    tiles = [
        jnp.where(ids == lane + float(LANES * t), 1.0, 0.0).astype(BF16)
        for t in range(width // LANES)
    ]
    return jnp.concatenate(tiles, axis=1)


def activation(linear):
    squashed = 1.0 / (1.0 + jnp.exp(-linear))
    return linear * squashed, squashed * (1.0 + linear * (1.0 - squashed))


def fused(
    n, quarter, edge_scale, node_scale,
    nf_any, ef_any, nc_any, ec_any, wi_any, bi_any, wo_any, bo_any, wn_any, bn_any, wq_any,
    ends_any, live_any, lists_any, counts_any, mult_any,
    ng_ref, eg_ref, gwi_ref, gbi_ref, gwo_ref, gbo_ref, gwn_ref, gbn_ref, gwq_ref, gbq_ref,
    col_s, col_t, tab_t, tab_tt, pick, pick_t, slope_s, hid_s, eb_s, cot_s, ecot_s,
    inv_s, agg_s, out1, in1, out2, in2,
    nf_ref, ef_ref, nc_ref, ec_ref, wi_ref, bi_ref, wo_ref, bo_ref, wn_ref, bn_ref, wq_ref,
    ends_ref, lists_ref, counts_ref, mult_ref, in_sem, out_sem, bias_s, bias_l,
    px_send, px_recv, pair_send, pair_recv, rs_send, rs_recv, ag_send, ag_recv, bs_send, bs_recv,
    *buffers,
):
    nodes = nf_ref.shape[0]
    d = nf_ref.shape[1]
    slots = nodes // NPE
    edges = ends_ref.shape[1]
    me = lax.axis_index("dom")
    rep = lax.axis_index("rep")
    offsets = (1, -1, quarter, -quarter)
    order = _axis_order
    ch = divisor_up_to(edges, 448)
    n_ch = edges // ch

    def device(index):
        return tuple(index if name == "dom" else rep for name in order)

    half = n // 2
    place, parity = me // 2, lax.rem(me, 2)
    kinds = len(buffers) // 4
    parts, pair_land, lands, fulls = (buffers[i * kinds : (i + 1) * kinds] for i in range(4))
    sources = (
        ends_any, nf_any, wi_any, bi_any, ef_any, wo_any, bo_any, counts_any, lists_any,
        mult_any, wq_any, wn_any, bn_any, nc_any, ec_any,
    )
    targets = (
        ends_ref, nf_ref, wi_ref, bi_ref, ef_ref, wo_ref, bo_ref, counts_ref, lists_ref,
        mult_ref, wq_ref, wn_ref, bn_ref, nc_ref, ec_ref,
    )
    loads = [
        pltpu.make_async_copy(source, target, in_sem.at[i])
        for i, (source, target) in enumerate(zip(sources, targets))
    ]
    for load in loads:
        load.start()

    def arrive(first, last):
        for load in loads[first:last]:
            load.wait()

    barrier = pltpu.get_barrier_semaphore()

    def greet(i, carry):
        pl.semaphore_signal(
            barrier, inc=1, device_id=device(lax.rem(me + i, n)), device_id_type=MESH
        )
        return carry

    lax.fori_loop(1, n, greet, 0)

    arrive(0, 1)
    ends = ends_ref[...].astype(F32)
    for start in range(0, edges, LANES):
        stop = min(start + LANES, edges)
        col_s[start:stop, :] = columns_of(ends[0:1, start:stop])
        col_t[start:stop, :] = columns_of(ends[1:2, start:stop])
    arrive(1, 9)
    s_count = lists_ref.shape[1]
    lane_row = lax.broadcasted_iota(jnp.int32, (1, s_count), 1)
    lists = []
    for k in range(4):
        row = jnp.where(lane_row < counts_ref[:, k : k + 1], lists_ref[k : k + 1, :], -1)
        lists.append(row.astype(F32))
    wi = wi_ref[...]
    ef_rows = lambda e, c: pl.ds(pl.multiple_of(e * edges + c * ch, 16), ch)
    nf2 = jnp.concatenate([nf_ref[e * NPE : (e + 1) * NPE, :] for e in range(slots)], axis=1)

    def forward(c, carry):
        rows = pl.ds(pl.multiple_of(c * ch, 16), ch)
        table = hits(col_t[rows, :], NPE)
        tab_t[rows, :] = table
        target = mm(table, nf2).astype(BF16)
        source = mm(hits(col_s[rows, :], NPE), nf2).astype(BF16)
        for e in range(slots):
            span = slice(e * d, (e + 1) * d)
            here = ef_rows(e, c)
            joined = jnp.concatenate([source[:, span], target[:, span], ef_ref[here, :]], axis=1)
            hidden, slope = activation(mm(joined, wi) + bi_ref[...])
            hid_s[here, :] = hidden.astype(BF16)
            slope_s[here, :] = slope
        return carry

    lax.fori_loop(0, n_ch, forward, 0)

    target_row = ends[1:2, :]
    nb = 128
    deg = []
    for b in range(NPE // nb):
        node_id = (lax.broadcasted_iota(jnp.int32, (nb, edges), 0) + b * nb).astype(F32)
        hit = jnp.where(target_row == node_id, 1.0, 0.0)
        tab_tt[b * nb : (b + 1) * nb, :] = hit.astype(BF16)
        deg.append(jnp.sum(hit, axis=1, keepdims=True))
    deg = jnp.concatenate(deg, axis=0)
    stacked = lambda ref: jnp.concatenate(
        [ref[e * edges : (e + 1) * edges, :] for e in range(slots)], axis=1
    )
    wo = wo_ref[...]
    wo2 = jnp.concatenate([wo, wo], axis=0)
    sum_e = mm(tab_tt[...], stacked(ef_ref))
    sum_h = mm(tab_tt[...], stacked(hid_s))
    for e in range(slots):
        span = slice(e * d, (e + 1) * d)
        pair = jnp.concatenate(halves(sum_h[:, span]), axis=1)
        agg_s[e * NPE : (e + 1) * NPE, :] = sum_e[:, span] + mm(pair, wo2) + deg * bo_ref[...]
    for k in range(4):
        pick[k * s_count : (k + 1) * s_count, :] = hits(columns_of(lists[k]), nodes)

    def partner_copies(out, incoming, which):
        return [
            pltpu.make_async_remote_copy(
                src_ref=out.at[k],
                dst_ref=incoming.at[k ^ 1],
                send_sem=px_send.at[which, k],
                recv_sem=px_recv.at[which, k ^ 1],
                device_id=device(lax.rem(me + offsets[k] + n, n)),
                device_id_type=MESH,
            )
            for k in range(4)
        ]

    def send_shared(values, out, incoming, which):
        pair = jnp.concatenate(halves(values), axis=1)
        copies = partner_copies(out, incoming, which)
        for k in range(4):
            both = mm(pick[k * s_count : (k + 1) * s_count, :], pair)
            out[k] = both[:, :d] + both[:, d:]
            copies[k].start()
        return copies

    def take_shared(values, incoming, copies):
        for k in range(4):
            copies[k].wait()
        moved = jnp.concatenate(
            halves(jnp.concatenate([incoming[k] for k in range(4)], axis=0)), axis=1
        )
        both = mm(pick_t[...], moved)
        return values + both[:, :d] + both[:, d:]

    pl.semaphore_wait(barrier, n - 1)
    copies = send_shared(agg_s[...], out1, in1, 0)

    for k in range(4):
        node_id = lax.broadcasted_iota(jnp.int32, (nodes, s_count), 0).astype(F32)
        pick_t[:, k * s_count : (k + 1) * s_count] = jnp.where(
            lists[k] == node_id, 1.0, 0.0
        ).astype(BF16)
    arrive(9, 14)
    mult = mult_ref[...].astype(F32)
    for b in range(nodes // LANES):
        inv_s[b * LANES : (b + 1) * LANES, :] = 1.0 / columns_of(mult[b : b + 1, :])
    live = live_any[0]
    slot_of = lax.broadcasted_iota(jnp.int32, (nodes, d), 0) // NPE
    node_cot = jnp.where(slot_of < live, nc_ref[...].astype(F32), 0.0)
    cot_n = node_cot.astype(BF16)
    hidden_back = mm_rt(cot_n, wq_ref[...])
    wn = wn_ref[...]
    early = mm(nf_ref[...], wn[:d, :]) + bn_ref[...]
    bias_s[...] = jnp.zeros_like(bias_s)
    bias_s[3:4, :] = jnp.sum(node_cot, axis=0, keepdims=True)

    consistent = (take_shared(agg_s[...], in1, copies) * inv_s[...]).astype(BF16)
    node_hidden, node_slope = activation(early + mm(consistent, wn[d:, :]))
    node_back32 = hidden_back * node_slope
    node_back = node_back32.astype(BF16)
    back = mm_rt(node_back, wn[d:, :]) * inv_s[...]
    agg_s[...] = back
    copies = send_shared(back, out2, in2, 1)

    def pair_copy(which):
        return pltpu.make_async_remote_copy(
            src_ref=parts[which].at[1 - parity],
            dst_ref=pair_land[which],
            send_sem=pair_send.at[0, which],
            recv_sem=pair_recv.at[0, which],
            device_id=device(2 * place + 1 - parity),
            device_id_type=MESH,
        )

    def reduce_copy(which, i):
        peer = lax.rem(place + i, half)
        return pltpu.make_async_remote_copy(
            src_ref=parts[which].at[parity, peer],
            dst_ref=lands[which].at[i - 1],
            send_sem=rs_send.at[which, i - 1],
            recv_sem=rs_recv.at[which, i - 1],
            device_id=device(2 * peer + parity),
            device_id_type=MESH,
        )

    def gather_copy(which, i, slot):
        peer = lax.rem(place + i, half)
        return pltpu.make_async_remote_copy(
            src_ref=fulls[which].at[parity, slot],
            dst_ref=fulls[which].at[parity, slot],
            send_sem=ag_send.at[which, i - 1],
            recv_sem=ag_recv.at[which, i - 1],
            device_id=device(2 * peer + parity),
            device_id_type=MESH,
        )

    def pair_back(which, side):
        return pltpu.make_async_remote_copy(
            src_ref=fulls[which].at[side],
            dst_ref=fulls[which].at[side],
            send_sem=pair_send.at[1, which],
            recv_sem=pair_recv.at[1, which],
            device_id=device(2 * place + 1 - parity),
            device_id_type=MESH,
        )

    def each(step):
        lax.fori_loop(1, half, lambda i, x: (step(i), x)[1], 0)

    def stage_one(which):
        pair_copy(which).start()

    def stage_two(which):
        pair_copy(which).wait()
        parts[which][parity] = parts[which][parity] + pair_land[which][...]
        each(lambda i: reduce_copy(which, i).start())

    def stage_three(which):
        def add(i, total):
            reduce_copy(which, i).wait()
            return total + lands[which][i - 1]

        fulls[which][parity, place] = lax.fori_loop(1, half, add, parts[which][parity, place])
        each(lambda i: gather_copy(which, i, place).start())

    def stage_four(which):
        def one(i):
            gather_copy(which, i, place).wait_send()
            gather_copy(which, i, lax.rem(place - i + half, half)).wait_recv()

        each(one)
        pair_back(which, parity).start()

    def stage_five(which):
        pair_back(which, parity).wait_send()
        pair_back(which, 1 - parity).wait_recv()

    def fill(which, first, value):
        part = parts[which]
        chunk = part.shape[2]
        rows = value.shape[0]
        for p in range(n):
            lo, hi = max(p * chunk, first), min((p + 1) * chunk, first + rows)
            if lo < hi:
                part[p // half, p % half, lo - p * chunk : hi - p * chunk, :] = value[
                    lo - first : hi - first, :
                ]

    def clear_tail(which, rows):
        part = parts[which]
        for p in range(n):
            if (p + 1) * part.shape[2] > rows:
                part[p // half, p % half] = jnp.zeros(part.shape[2:], F32)

    def unfill(which, first, rows):
        full = fulls[which]
        chunk = full.shape[2]
        pieces = []
        for p in range(n):
            lo, hi = max(p * chunk, first), min((p + 1) * chunk, first + rows)
            if lo < hi:
                pieces.append(full[p // half, p % half, lo - p * chunk : hi - p * chunk, :])
        return jnp.concatenate(pieces, axis=0)

    for which in range(kinds):
        clear_tail(which, 3 * d if which == 0 else d)
    node_input = jnp.concatenate([nf_ref[...], consistent], axis=1)
    fill(0, 0, mm_lt(node_input, node_back))
    fill(0, 2 * d, mm_lt(node_hidden.astype(BF16), cot_n))
    bias_s[2:3, :] = jnp.sum(node_back.astype(F32), axis=0, keepdims=True)
    stage_one(0)
    node_base = node_cot + mm_rt(node_back, wn[:d, :])

    agg_back = take_shared(agg_s[...], in2, copies)
    stage_two(0)
    arrive(14, 15)
    highs, lows = halves(agg_back)
    quad = jnp.concatenate(
        [highs[e * NPE : (e + 1) * NPE, :] for e in range(slots)]
        + [lows[e * NPE : (e + 1) * NPE, :] for e in range(slots)],
        axis=1,
    )

    def backward(c, sums):
        rows = pl.ds(pl.multiple_of(c * ch, 16), ch)
        got = mm(tab_t[rows, :], quad)
        for e in range(slots):
            here = ef_rows(e, c)
            given = jnp.where(
                jnp.broadcast_to(live, (ch, d)) > e, ec_ref[here, :].astype(F32), 0.0
            )
            cot = given + (got[:, e * d : (e + 1) * d] + got[:, (slots + e) * d : (slots + e + 1) * d])
            ecot_s[here, :] = cot
            half = cot.astype(BF16)
            cot_s[here, :] = half
            eb = (mm_rt(half, wo) * slope_s[here, :]).astype(BF16)
            eb_s[here, :] = eb
            sums = (
                sums[0] + jnp.sum(eb.astype(F32), axis=0, keepdims=True),
                sums[1] + jnp.sum(half.astype(F32), axis=0, keepdims=True),
            )
        return sums

    zero = jnp.zeros((1, d), F32)
    sums = lax.fori_loop(0, n_ch, backward, (zero, zero))
    bias_s[0:1, :] = sums[0]
    bias_s[1:2, :] = sums[1]

    def bias_copy(i):
        return pltpu.make_async_remote_copy(
            src_ref=bias_s,
            dst_ref=bias_l.at[i - 1],
            send_sem=bs_send.at[i - 1],
            recv_sem=bs_recv.at[i - 1],
            device_id=device(lax.rem(me + i, n)),
            device_id_type=MESH,
        )

    fill(1, 0, mm_lt(hid_s[...], cot_s[...]))
    stage_one(1)
    stage_three(0)
    lax.fori_loop(1, n, lambda i, x: (bias_copy(i).start(), x)[1], 0)

    fill(2, 0, mm_lt(ef_ref[...], eb_s[...]))
    stage_one(2)
    eb2 = stacked(eb_s)
    unstack = lambda v: jnp.concatenate(
        [v[:, e * d : (e + 1) * d] for e in range(slots)], axis=0
    )
    by_target = jnp.concatenate(halves(unstack(mm(tab_tt[...], eb2))), axis=1)
    grads = mm_lt(nf_ref[...], by_target)
    fill(3, 0, grads[:, :d] + grads[:, d:])
    stage_one(3)
    stage_two(1)
    source_row = ends[0:1, :]
    node_id = lax.broadcasted_iota(jnp.int32, (NPE, edges), 0).astype(F32)
    source_hit = jnp.where(source_row == node_id, 1.0, 0.0).astype(BF16)
    by_source = jnp.concatenate(halves(unstack(mm(source_hit, eb2))), axis=1)
    grads = mm_lt(nf_ref[...], by_source)
    fill(4, 0, grads[:, :d] + grads[:, d:])
    stage_one(4)
    stage_two(2)
    stage_two(3)
    stage_four(0)

    ws, wt = wi[:d, :], wi[d : 2 * d, :]
    w4 = jnp.concatenate([ws, ws, wt, wt], axis=1)
    spread = jnp.concatenate([by_source, by_target], axis=1)
    ng_ref[...] = (node_base + mm_rt(spread, w4)).astype(BF16)
    stage_two(4)
    stage_three(1)
    we = wi[2 * d :, :]

    def last(c, carry):
        rows = pl.ds(pl.multiple_of(c * ch, 16), ch)
        eg_ref[rows, :] = (ecot_s[rows, :] + mm_rt(eb_s[rows, :], we)).astype(BF16)
        return carry

    lax.fori_loop(0, n_ch * slots, last, 0)
    stage_three(2)
    stage_three(3)
    stage_three(4)

    def add_bias(i, total):
        bias_copy(i).wait()
        return total + bias_l[i - 1]

    bias = lax.fori_loop(1, n, add_bias, bias_s[...])
    gbi_ref[...] = bias[0:1, :] * edge_scale
    gbo_ref[...] = bias[1:2, :] * edge_scale
    gbn_ref[...] = bias[2:3, :] * node_scale
    gbq_ref[...] = bias[3:4, :] * node_scale
    for which in range(1, kinds):
        stage_four(which)
    stage_five(0)
    gwn_ref[...] = unfill(0, 0, 2 * d) * node_scale
    gwq_ref[...] = unfill(0, 2 * d, d) * node_scale
    stage_five(1)
    gwo_ref[...] = unfill(1, 0, d) * edge_scale
    for which, first in ((2, 2 * d), (3, d), (4, 0)):
        stage_five(which)
        gwi_ref[first : first + d, :] = unfill(which, 0, d) * edge_scale


def deliver(*refs):
    count = len(refs) // 2
    sems = refs[-1]
    copies = [
        pltpu.make_async_copy(refs[i], refs[count + i], sems.at[i]) for i in range(count)
    ]
    for copy in copies:
        copy.start()
    for copy in copies:
        copy.wait()


_axis_order = ("dom", "rep")


def body(
    node_features, edge_features, node_cotangent, edge_cotangent,
    edge_in_weight, edge_in_bias, edge_out_weight, edge_out_bias,
    node_in_weight, node_in_bias, node_out_weight,
    edge_ends, live_elements, shared_nodes, shared_counts, multiplicity,
):
    n = lax.axis_size("dom")
    nodes, d = node_features.shape
    rows = edge_features.shape[0]
    edges = edge_ends.shape[1]
    s_count = shared_nodes.shape[2]
    hid = edge_in_weight.shape[1]
    edge_scale = 1.0 / math.sqrt(rows * n)
    node_scale = 1.0 / math.sqrt(nodes * n)
    chunk = lambda total: -(-total // (8 * n)) * 8
    chunks = [chunk(3 * d)] + [chunk(d)] * 4
    half = n // 2
    vmem = pl.BlockSpec(memory_space=pltpu.VMEM)
    raw = pl.BlockSpec(memory_space=pl.ANY)
    hbm = pl.BlockSpec(memory_space=pltpu.HBM)
    shape = jax.ShapeDtypeStruct
    dma = pltpu.SemaphoreType.DMA
    vshape = pltpu.VMEM
    row = vshape((1, d), F32)
    args = (
        node_features, edge_features, node_cotangent, edge_cotangent,
        edge_in_weight, edge_in_bias.reshape(1, -1), edge_out_weight, edge_out_bias.reshape(1, -1),
        node_in_weight, node_in_bias.reshape(1, -1), node_out_weight,
        edge_ends, live_elements, shared_nodes[0], shared_counts,
        multiplicity.reshape(-1, LANES),
    )

    outs = pl.pallas_call(
        functools.partial(fused, n, n // 4, edge_scale, node_scale),
        out_shape=(
            vshape((nodes, d), BF16), vshape((rows, d), BF16),
            vshape((3 * d, hid), F32), row, vshape((hid, d), F32), row,
            vshape((2 * d, hid), F32), row, vshape((hid, d), F32), row,
        ),
        in_specs=[hbm] * 12 + [pl.BlockSpec(memory_space=pltpu.SMEM)] + [hbm] * 3,
        out_specs=(vmem,) * 10,
        scratch_shapes=[
            pltpu.VMEM((edges, LANES), F32), pltpu.VMEM((edges, LANES), F32),
            pltpu.VMEM((edges, NPE), BF16), pltpu.VMEM((NPE, edges), BF16),
            pltpu.VMEM((4 * s_count, nodes), BF16), pltpu.VMEM((nodes, 4 * s_count), BF16),
            pltpu.VMEM((rows, hid), F32), pltpu.VMEM((rows, hid), BF16),
            pltpu.VMEM((rows, hid), BF16), pltpu.VMEM((rows, d), BF16), pltpu.VMEM((rows, d), F32),
            pltpu.VMEM((nodes, d), F32), pltpu.VMEM((nodes, d), F32),
        ]
        + [pltpu.VMEM((4, s_count, d), F32)] * 4
        + [pltpu.VMEM(arg.shape, arg.dtype) for i, arg in enumerate(args) if i != 12]
        + [dma((len(args),)), dma((2,))]
        + [pltpu.VMEM((8, d), F32), pltpu.VMEM((n - 1, 8, d), F32)]
        + [dma((2, 4)), dma((2, 4))]
        + [dma((2, len(chunks)))] * 2
        + [dma((len(chunks), half - 1))] * 4
        + [dma((n - 1,))] * 2
        + [pltpu.VMEM((2, half, c, d), F32) for c in chunks]
        + [pltpu.VMEM((half, c, d), F32) for c in chunks]
        + [pltpu.VMEM((half - 1, c, d), F32) for c in chunks]
        + [pltpu.VMEM((2, half, c, d), F32) for c in chunks],
        compiler_params=pltpu.CompilerParams(
            collective_id=0, has_side_effects=True, vmem_limit_bytes=60 << 20
        ),
    )(*args)
    outs = pl.pallas_call(
        deliver,
        out_shape=tuple(shape(out.shape, out.dtype) for out in outs),
        in_specs=[vmem] * len(outs),
        out_specs=(raw,) * len(outs),
        scratch_shapes=[dma((len(outs),))],
        compiler_params=pltpu.CompilerParams(vmem_limit_bytes=8 << 20),
    )(*outs)
    flat = lambda v: v.reshape(-1)
    return (
        outs[0], outs[1], outs[2], flat(outs[3]), outs[4], flat(outs[5]),
        outs[6], flat(outs[7]), outs[8], flat(outs[9]),
    )


def solution(mesh):
    global _axis_order
    _axis_order = tuple(mesh.axis_names)
    both = P(("rep", "dom"))
    both2 = P(("rep", "dom"), None)
    in_specs = (
        (both2,) * 4 + (P(),) * 8 + (both, P(("rep", "dom"), None, None), both2, both)
    )
    out_specs = (both2, both2) + (P("rep", None), P("rep")) * 4
    return jax.shard_map(body, mesh=mesh, in_specs=in_specs, out_specs=out_specs, check_vma=False)
```

```python
import functools
import math

import jax
import jax.numpy as jnp
from jax import lax
from jax.experimental import pallas as pl
from jax.experimental.pallas import tpu as pltpu
from jax.sharding import PartitionSpec as P

NPE = 512
LANES = 128
F32 = jnp.float32
BF16 = jnp.bfloat16
MESH = pl.DeviceIdType.MESH
CHUNK = 448


def divisor_up_to(total, cap):
    best = 16
    for size in range(16, cap + 1, 16):
        if total % size == 0:
            best = size
    return best


def mm(left, right):
    return lax.dot_general(left, right, (((1,), (0,)), ((), ())), preferred_element_type=F32)


def half_of(rows):
    return rows // 32 * 16


def in_two(step, left, right):
    cut = half_of(left.shape[0])
    return jnp.concatenate([step(left[:cut, :], right), step(left[cut:, :], right)], axis=0)


def mm2(left, right):
    return in_two(mm, left, right)


def mm_rt2(left, right):
    return in_two(mm_rt, left, right)


def mm_lt2(left, right):
    cut = half_of(left.shape[0])
    return mm_lt(left[:cut, :], right[:cut, :]) + mm_lt(left[cut:, :], right[cut:, :])


def mm_rt(left, right):
    return lax.dot_general(left, right, (((1,), (1,)), ((), ())), preferred_element_type=F32)


def mm_lt(left, right):
    return lax.dot_general(left, right, (((0,), (0,)), ((), ())), preferred_element_type=F32)


def halves(value):
    high = value.astype(BF16)
    low = (value - high.astype(F32)).astype(BF16)
    return high, low


def columns_of(row):
    return jnp.transpose(jnp.broadcast_to(row, (LANES, row.shape[1])))


def hits(ids, width, shift=0):
    lane = lax.broadcasted_iota(jnp.int32, ids.shape, 1).astype(F32)
    moved = ids + float(shift) if shift else ids
    tiles = [
        jnp.where(moved == lane + float(LANES * t + shift), 1.0, 0.0).astype(BF16)
        for t in range(width // LANES)
    ]
    return jnp.concatenate(tiles, axis=1)


def row_hits(row, height, shift=0):
    node = (lax.broadcasted_iota(jnp.int32, (height, row.shape[1]), 0) + shift).astype(F32)
    return jnp.where(row + float(shift) == node, 1.0, 0.0).astype(BF16)


def repeated(weight, times):
    rows, cols = weight.shape
    zero = jnp.zeros((rows, cols), weight.dtype)
    return jnp.concatenate(
        [
            jnp.concatenate([weight if a == b else zero for b in range(times)], axis=1)
            for a in range(times)
        ],
        axis=0,
    )


def activation(linear):
    squashed = 0.5 * jnp.tanh(0.5 * linear) + 0.5
    return linear * squashed, squashed * (1.0 + linear * (1.0 - squashed))


def fused(
    n, quarter, edge_scale, node_scale,
    nf_any, ef_any, nc_any, ec_any, wi_any, bi_any, wo_any, bo_any, wn_any, bn_any, wq_any,
    ends_any, live_any, lists_any, counts_any, mult_any,
    ng_ref, eg_ref, gwi_ref, gbi_ref, gwo_ref, gbo_ref, gwn_ref, gbn_ref, gwq_ref, gbq_ref,
    col_s, col_t, lcol, rows_s, deg_s, src_s, tgt_s, hid_s, slope_s, lin_s, giv_s, join_t, eb_s,
    sum_s, sum_t, pick_t, gwo_s, cot_s, hback_s, early_s, base_s, inv_s, agg_s,
    out1, in1, out2, in2,
    nf_ref, ef_ref, nc_ref, ec_ref, wi_ref, bi_ref, wo_ref, bo_ref, wn_ref, bn_ref, wq_ref,
    ends_ref, lists_ref, counts_ref, mult_ref, in_sem, bias_s, bias_l,
    px_send, px_recv, bs_send, bs_recv,
    qparts, qlands, mids, clands, qs_send, qs_recv, cs_send, cs_recv, gs_send, gs_recv,
):
    nodes = nf_ref.shape[0]
    d = nf_ref.shape[1]
    slots = nodes // NPE
    wide = slots * d
    edges = ends_ref.shape[1]
    me = lax.axis_index("dom")
    rep = lax.axis_index("rep")
    offsets = (1, -1, quarter, -quarter)
    order = _axis_order
    ch = divisor_up_to(edges, CHUNK)
    n_ch = edges // ch

    def device(index):
        return tuple(index if name == "dom" else rep for name in order)

    team, seat = me // 4, lax.rem(me, 4)
    teams = n // 4
    groups = (
        ((ends_any, ends_ref),),
        ((nf_any, nf_ref), (wi_any, wi_ref), (bi_any, bi_ref), (ef_any, ef_ref)),
        ((lists_any, lists_ref), (counts_any, counts_ref)),
        ((wo_any, wo_ref), (bo_any, bo_ref)),
        (
            (mult_any, mult_ref), (wq_any, wq_ref), (wn_any, wn_ref), (bn_any, bn_ref),
            (nc_any, nc_ref), (ec_any, ec_ref),
        ),
    )
    loads = []
    count = 0
    for group in groups:
        loads.append([])
        for source, target in group:
            loads[-1].append(pltpu.make_async_copy(source, target, in_sem.at[count]))
            loads[-1][-1].start()
            count += 1

    def arrive(which):
        for load in loads[which]:
            load.wait()

    barrier = pltpu.get_barrier_semaphore()

    def greet(i, carry):
        pl.semaphore_signal(
            barrier, inc=1, device_id=device(lax.rem(me + i, n)), device_id_type=MESH
        )
        return carry

    lax.fori_loop(1, n, greet, 0)

    arrive(0)
    ends = ends_ref[...].astype(F32)
    source_row, target_row = ends[0:1, :], ends[1:2, :]
    for start in range(0, edges, LANES):
        stop = min(start + LANES, edges)
        col_t[start:stop, :] = columns_of(ends[1:2, start:stop])
        col_s[start:stop, :] = columns_of(ends[0:1, start:stop])
    arrive(1)
    wi = wi_ref[...]
    ws, wt, we = wi[:d, :], wi[d : 2 * d, :], wi[2 * d :, :]
    by_slot = lambda v: jnp.concatenate(
        [v[e * NPE : (e + 1) * NPE, :] for e in range(slots)], axis=1
    )
    by_row = lambda v: jnp.concatenate(
        [v[:, e * d : (e + 1) * d] for e in range(slots)], axis=0
    )
    fold = lambda v: v[:, :d] + v[:, d:]
    pair_of = lambda v: jnp.concatenate(halves(v), axis=1)
    across = lambda ref, first, count, step: jnp.concatenate(
        [ref[e * step + first : e * step + first + count, :] for e in range(slots)], axis=1
    )
    twice = lambda v: jnp.concatenate([v] * slots, axis=1)
    nf2 = by_slot(nf_ref[...])
    w_in = jnp.concatenate([repeated(w, slots) for w in (ws, wt, we)], axis=0)
    bi_wide = twice(bi_ref[...])

    for c in range(n_ch):
        rows = slice(c * ch, (c + 1) * ch)
        target = mm(hits(col_t[rows, :], NPE), nf2).astype(BF16)
        source = mm(hits(col_s[rows, :], NPE), nf2).astype(BF16)
        src_s[rows, :] = source
        tgt_s[rows, :] = target
        joined = jnp.concatenate([source, target, across(ef_ref, c * ch, ch, edges)], axis=1)
        hidden, slope = activation(mm2(joined, w_in) + bi_wide)
        hid_s[rows, :] = hidden.astype(BF16)
        slope_s[rows, :] = slope

    arrive(2)
    s_count = lists_ref.shape[1]
    lane_row = lax.broadcasted_iota(jnp.int32, (1, s_count), 1)
    for k in range(4):
        row = jnp.where(
            lane_row < counts_ref[:, k : k + 1], lists_ref[k : k + 1, :], -1
        ).astype(F32)
        rows_s[k] = jnp.broadcast_to(row, (8, s_count))
        lcol[k * s_count : (k + 1) * s_count, :] = columns_of(row)
    arrive(3)
    wo = wo_ref[...]
    wo_wide = repeated(wo, slots)
    nb = 128
    for b in range(NPE // nb):
        node_id = (lax.broadcasted_iota(jnp.int32, (nb, edges), 0) + b * nb).astype(F32)
        deg_s[b * nb : (b + 1) * nb, :] = jnp.broadcast_to(
            jnp.sum(jnp.where(target_row == node_id, 1.0, 0.0), axis=1, keepdims=True), (nb, d)
        )
    sums = mm(
        row_hits(target_row, NPE),
        jnp.concatenate([across(ef_ref, 0, edges, edges), hid_s[...]], axis=1),
    )
    sum_s[...] = sums[:, wide:]
    agg2 = (
        sums[:, :wide]
        + mm2(pair_of(sums[:, wide:]), jnp.concatenate([wo_wide, wo_wide], axis=0))
        + twice(deg_s[...] * bo_ref[...])
    )
    agg_s[...] = by_row(agg2)

    upper = me >= n // 2
    turns = [jnp.where(upper, a, b) for a, b in ((2, 3), (0, 1), (3, 2), (1, 0))]
    steps = [jnp.where(upper, offsets[a], offsets[b]) for a, b in ((2, 3), (0, 1), (3, 2), (1, 0))]

    def partner_copy(out, incoming, which, j):
        k = turns[j]
        other = k + 1 - 2 * lax.rem(k, 2)
        return pltpu.make_async_remote_copy(
            src_ref=out.at[k],
            dst_ref=incoming.at[other],
            send_sem=px_send.at[which],
            recv_sem=px_recv.at[which, other],
            device_id=device(lax.rem(me + steps[j] + n, n)),
            device_id_type=MESH,
        )

    def landing(out, incoming, which, j):
        k = turns[j]
        return pltpu.make_async_remote_copy(
            src_ref=out.at[k],
            dst_ref=incoming.at[k],
            send_sem=px_send.at[which],
            recv_sem=px_recv.at[which, k],
            device_id=device(lax.rem(me + 1, n)),
            device_id_type=MESH,
        )

    def send_shared(values, out, incoming, which):
        pair = pair_of(values)
        for k in range(4):
            out[k] = fold(
                mm(hits(lcol[k * s_count : (k + 1) * s_count, :], nodes, which), pair)
            )
        for j in range(4):
            partner_copy(out, incoming, which, j).start()

    def landed(out, incoming, which, js):
        for j in js:
            landing(out, incoming, which, j).wait_recv()
        moved = jnp.concatenate([incoming[turns[j]] for j in js], axis=0)
        entries = jnp.concatenate([rows_s[turns[j]][0:1, :] for j in js], axis=1)
        return pair_of(moved), entries

    near, far = (2, 3), (0, 1)
    pl.semaphore_wait(barrier, n - 1)
    send_shared(agg_s[...], out1, in1, 0)

    arrive(4)
    mult = mult_ref[...].astype(F32)
    for b in range(nodes // LANES):
        inv_s[b * LANES : (b + 1) * LANES, :] = 1.0 / columns_of(mult[b : b + 1, :])
    live = live_any[0]
    slot_of = lax.broadcasted_iota(jnp.int32, (nodes, d), 0) // NPE
    node_cot = jnp.where(slot_of < live, nc_ref[...].astype(F32), 0.0)
    cot_s[...] = node_cot.astype(BF16)
    wn = wn_ref[...]
    wn_wide = repeated(wn[d:, :], slots)
    hback_s[...] = mm_rt2(by_slot(cot_s[...]), repeated(wq_ref[...], slots))
    early_s[...] = mm2(nf2, repeated(wn[:d, :], slots)) + twice(bn_ref[...])
    bias_s[...] = jnp.zeros_like(bias_s)
    bias_s[3:4, :] = jnp.sum(node_cot, axis=0, keepdims=True)

    given_sum = jnp.zeros((1, d), F32)
    gwo = jnp.zeros((d, d), F32)
    for e in range(slots):
        lanes = slice(e * d, (e + 1) * d)
        given = jnp.where(
            jnp.broadcast_to(live, (edges, d)) > e,
            ec_ref[e * edges : (e + 1) * edges, :].astype(F32),
            0.0,
        )
        given_sum = given_sum + jnp.sum(given, axis=0, keepdims=True)
        giv_s[:, lanes] = given.astype(BF16)
        gwo = gwo + mm_lt(hid_s[:, lanes], giv_s[:, lanes])
    gwo_s[...] = gwo
    lin_s[...] = mm_rt2(giv_s[...], wo_wide)
    for at, block in enumerate((src_s[...], tgt_s[...], across(ef_ref, 0, edges, edges))):
        join_t[at * wide : (at + 1) * wide, :] = jnp.transpose(block)
    sum_rows = pair_of(by_row(sum_s[...]))
    picked = fold(mm2(hits(lcol[...], nodes, 2), sum_rows))
    pick_t[...] = jnp.transpose(pair_of(picked))
    sum_t[...] = jnp.transpose(sum_rows)

    def gather_in(js):
        moved, entries = landed(out1, in1, 0, js)
        return agg_s[...] + fold(mm2(row_hits(entries, nodes), moved))

    agg_s[...] = gather_in(near)
    consistent = (gather_in(far) * inv_s[...]).astype(BF16)
    node_hidden, node_slope = activation(early_s[...] + mm2(by_slot(consistent), wn_wide))
    node_back2 = (hback_s[...] * node_slope).astype(BF16)
    back = by_row(mm_rt2(node_back2, wn_wide)) * inv_s[...]
    agg_s[...] = back
    send_shared(back, out2, in2, 1)

    quart = qparts.shape[2]
    results = (
        (gwn_ref, 0, node_scale), (gwn_ref, d, node_scale), (gwq_ref, 0, node_scale),
        (gwo_ref, 0, edge_scale),
        (gwi_ref, 2 * d, edge_scale), (gwi_ref, d, edge_scale), (gwi_ref, 0, edge_scale),
    )

    def seat_of(i):
        return lax.rem(seat + i, 4)

    def split_copy(p, i):
        return pltpu.make_async_remote_copy(
            src_ref=qparts.at[p, seat_of(i)],
            dst_ref=qlands.at[p, i - 1],
            send_sem=qs_send,
            recv_sem=qs_recv.at[p],
            device_id=device(4 * team + seat_of(i)),
            device_id_type=MESH,
        )

    def cross_copy(p, i):
        return pltpu.make_async_remote_copy(
            src_ref=mids.at[p],
            dst_ref=clands.at[p, i - 1],
            send_sem=cs_send,
            recv_sem=cs_recv.at[p],
            device_id=device(4 * lax.rem(team + i, teams) + seat),
            device_id_type=MESH,
        )

    def share_copy(p, i):
        ref, first, _ = results[p]
        rows = pl.ds(pl.multiple_of(first + seat * quart, 8), quart)
        return pltpu.make_async_remote_copy(
            src_ref=ref.at[rows],
            dst_ref=ref.at[rows],
            send_sem=gs_send,
            recv_sem=gs_recv,
            device_id=device(4 * team + seat_of(i)),
            device_id_type=MESH,
        )

    def whole(ref, send_sem, recv_sem):
        return pltpu.make_async_remote_copy(
            src_ref=ref,
            dst_ref=ref,
            send_sem=send_sem,
            recv_sem=recv_sem,
            device_id=device(lax.rem(me + 1, n)),
            device_id_type=MESH,
        )

    def hold(p, value):
        for j in range(4):
            qparts[p, j] = value[j * quart : (j + 1) * quart, :]

    def push(p):
        for i in (2, 1, 3):
            split_copy(p, i).start()

    def cross(p):
        whole(qlands.at[p], qs_send, qs_recv.at[p]).wait_recv()
        total = qparts[p, seat]
        for i in range(3):
            total = total + qlands[p, i]
        mids[p] = total
        for i in range(1, teams):
            cross_copy(p, i).start()

    def share(p):
        whole(clands.at[p], cs_send, cs_recv.at[p]).wait_recv()
        total = mids[p]
        for i in range(teams - 1):
            total = total + clands[p, i]
        ref, first, scale = results[p]
        ref[pl.ds(pl.multiple_of(first + seat * quart, 8), quart), :] = total * scale
        for i in (2, 1, 3):
            share_copy(p, i).start()

    node_back = by_row(node_back2)
    hold(0, mm_lt2(nf_ref[...], node_back))
    hold(1, mm_lt2(consistent, node_back))
    hold(2, mm_lt2(by_row(node_hidden.astype(BF16)), cot_s[...]))
    bias_s[2:3, :] = jnp.sum(node_back.astype(F32), axis=0, keepdims=True)
    base_s[...] = cot_s[...].astype(F32) + mm_rt2(node_back, wn[:d, :])
    wo_rows = jnp.concatenate([wo, wo], axis=1)
    pair_back = pair_of(back)
    crossed = mm2(sum_t[...], pair_back)
    gwo_s[...] = gwo_s[...] + fold(crossed[:d, :]) + fold(crossed[d:, :])
    spread_back = by_slot(mm_rt2(pair_back, wo_rows))
    for c in range(n_ch):
        rows = slice(c * ch, (c + 1) * ch)
        got = mm(hits(col_t[rows, :], NPE, 1), pair_of(spread_back))
        lin_s[rows, :] = lin_s[rows, :] + got[:, :wide] + got[:, wide:]

    for p in range(3):
        push(p)

    def toward(moved, entries, e):
        wanted = entries - float(NPE * e)
        marks = jnp.concatenate(
            [
                jnp.where(col_t[...] == wanted[:, t * LANES : (t + 1) * LANES], 1.0, 0.0).astype(BF16)
                for t in range(entries.shape[1] // LANES)
            ],
            axis=1,
        )
        return fold(mm(marks, moved))

    moved, entries = landed(out2, in2, 1, near)
    moved = pair_of(mm_rt2(moved, wo_rows))
    for e in range(slots):
        lanes = slice(e * d, (e + 1) * d)
        lin_s[:, lanes] = lin_s[:, lanes] + toward(moved, entries, e)
    moved, entries = landed(out2, in2, 1, far)
    moved = pair_of(mm_rt2(moved, wo_rows))
    for e in range(slots):
        lanes = slice(e * d, (e + 1) * d)
        eb_s[:, lanes] = (
            (lin_s[:, lanes] + toward(moved, entries, e)) * slope_s[:, lanes]
        ).astype(BF16)
    arrived = pair_of(jnp.concatenate([in2[k] for k in range(4)], axis=0))
    added = mm2(pick_t[...], arrived)
    hold(3, gwo_s[...] + fold(added[:d, :]) + fold(added[d:, :]))
    push(3)

    def weigh(at):
        total = None
        for e in range(slots):
            first = at * wide + e * d
            both = mm(join_t[first : first + d, :], eb_s[...])[:, e * d : (e + 1) * d]
            total = both if total is None else total + both
        return total

    for at in (2, 1, 0):
        hold(6 - at, weigh(at))
        push(6 - at)
    column = jnp.sum(eb_s[...].astype(F32), axis=0, keepdims=True)
    bias_row = column[:, :d]
    for e in range(1, slots):
        bias_row = bias_row + column[:, e * d : (e + 1) * d]
    bias_s[0:1, :] = bias_row
    entry_row = jnp.concatenate([rows_s[k][0:1, :] for k in range(4)], axis=1)
    agg_back = agg_s[...] + fold(mm2(row_hits(entry_row, nodes, 1), arrived))
    degrees = jnp.concatenate([deg_s[...]] * slots, axis=0)
    bias_s[1:2, :] = given_sum + jnp.sum(degrees * agg_back, axis=0, keepdims=True)

    def bias_copy(i):
        return pltpu.make_async_remote_copy(
            src_ref=bias_s,
            dst_ref=bias_l.at[i - 1],
            send_sem=bs_send,
            recv_sem=bs_recv,
            device_id=device(lax.rem(me + i, n)),
            device_id_type=MESH,
        )

    lax.fori_loop(1, n, lambda i, x: (bias_copy(i).start(), x)[1], 0)

    eb2 = eb_s[...]
    we_wide = repeated(we, slots)
    quad = pair_of(by_slot(agg_back))
    for c in range(n_ch):
        rows = slice(c * ch, (c + 1) * ch)
        got = mm(hits(col_t[rows, :], NPE, 2), quad)
        cot = giv_s[rows, :].astype(F32) + (got[:, :wide] + got[:, wide:])
        value = (cot + mm_rt(eb_s[rows, :], we_wide)).astype(BF16)
        for e in range(slots):
            eg_ref[e * edges + c * ch : e * edges + (c + 1) * ch, :] = value[
                :, e * d : (e + 1) * d
            ]
    for p in range(0, 4):
        cross(p)
    by_target = pair_of(by_row(mm2(row_hits(target_row, NPE, 1), eb2)))
    for p in range(4, 7):
        cross(p)
    by_source = pair_of(by_row(mm2(row_hits(source_row, NPE, 1), eb2)))
    w4 = jnp.concatenate([ws, ws, wt, wt], axis=1)
    spread = jnp.concatenate([by_source, by_target], axis=1)
    ng_ref[...] = (base_s[...] + mm_rt2(spread, w4)).astype(BF16)
    for p in range(7):
        share(p)

    whole(bias_l, bs_send, bs_recv).wait_recv()
    bias = lax.fori_loop(1, n, lambda i, total: total + bias_l[i - 1], bias_s[...])
    gbi_ref[...] = bias[0:1, :] * edge_scale
    gbo_ref[...] = bias[1:2, :] * edge_scale
    gbn_ref[...] = bias[2:3, :] * node_scale
    gbq_ref[...] = bias[3:4, :] * node_scale
    whole(bias_l, bs_send, bs_recv).wait_send()
    whole(in1, px_send.at[0], px_recv.at[0, 0]).wait_send()
    whole(in2, px_send.at[1], px_recv.at[1, 0]).wait_send()
    whole(qlands, qs_send, qs_recv.at[0]).wait_send()
    whole(clands, cs_send, cs_recv.at[0]).wait_send()
    whole(qlands, gs_send, gs_recv).wait()


def deliver(*refs):
    count = len(refs) // 2
    sems = refs[-1]
    copies = [
        pltpu.make_async_copy(refs[i], refs[count + i], sems.at[i]) for i in range(count)
    ]
    for copy in copies:
        copy.start()
    for copy in copies:
        copy.wait()


_axis_order = ("dom", "rep")


def body(
    node_features, edge_features, node_cotangent, edge_cotangent,
    edge_in_weight, edge_in_bias, edge_out_weight, edge_out_bias,
    node_in_weight, node_in_bias, node_out_weight,
    edge_ends, live_elements, shared_nodes, shared_counts, multiplicity,
):
    n = lax.axis_size("dom")
    nodes, d = node_features.shape
    rows = edge_features.shape[0]
    edges = edge_ends.shape[1]
    s_count = shared_nodes.shape[2]
    hid = edge_in_weight.shape[1]
    edge_scale = 1.0 / math.sqrt(rows * n)
    node_scale = 1.0 / math.sqrt(nodes * n)
    slots = nodes // NPE
    quart = d // 4
    teams = n // 4
    vmem = pl.BlockSpec(memory_space=pltpu.VMEM)
    raw = pl.BlockSpec(memory_space=pl.ANY)
    hbm = pl.BlockSpec(memory_space=pltpu.HBM)
    shape = jax.ShapeDtypeStruct
    dma = pltpu.SemaphoreType.DMA
    vshape = pltpu.VMEM
    row = vshape((1, d), F32)
    args = (
        node_features, edge_features, node_cotangent, edge_cotangent,
        edge_in_weight, edge_in_bias.reshape(1, -1), edge_out_weight, edge_out_bias.reshape(1, -1),
        node_in_weight, node_in_bias.reshape(1, -1), node_out_weight,
        edge_ends, live_elements, shared_nodes[0], shared_counts,
        multiplicity.reshape(-1, LANES),
    )

    outs = pl.pallas_call(
        functools.partial(fused, n, n // 4, edge_scale, node_scale),
        out_shape=(
            vshape((nodes, d), BF16), vshape((rows, d), BF16),
            vshape((3 * d, hid), F32), row, vshape((hid, d), F32), row,
            vshape((2 * d, hid), F32), row, vshape((hid, d), F32), row,
        ),
        in_specs=[hbm] * 12 + [pl.BlockSpec(memory_space=pltpu.SMEM)] + [hbm] * 3,
        out_specs=(vmem,) * 10,
        scratch_shapes=[
            pltpu.VMEM((edges, LANES), F32), pltpu.VMEM((edges, LANES), F32),
            pltpu.VMEM((4 * s_count, LANES), F32), pltpu.VMEM((4, 8, s_count), F32),
            pltpu.VMEM((NPE, d), F32),
            pltpu.VMEM((edges, slots * d), BF16), pltpu.VMEM((edges, slots * d), BF16),
            pltpu.VMEM((edges, slots * hid), BF16), pltpu.VMEM((edges, slots * hid), F32),
            pltpu.VMEM((edges, slots * hid), F32), pltpu.VMEM((edges, slots * d), BF16),
            pltpu.VMEM((3 * slots * d, edges), BF16), pltpu.VMEM((edges, slots * hid), BF16),
            pltpu.VMEM((NPE, slots * hid), F32), pltpu.VMEM((2 * hid, nodes), BF16),
            pltpu.VMEM((2 * hid, 4 * s_count), BF16), pltpu.VMEM((hid, d), F32),
            pltpu.VMEM((nodes, d), BF16), pltpu.VMEM((NPE, slots * hid), F32),
            pltpu.VMEM((NPE, slots * hid), F32), pltpu.VMEM((nodes, d), F32),
            pltpu.VMEM((nodes, d), F32), pltpu.VMEM((nodes, d), F32),
        ]
        + [pltpu.VMEM((4, s_count, d), F32)] * 4
        + [pltpu.VMEM(arg.shape, arg.dtype) for i, arg in enumerate(args) if i != 12]
        + [dma((len(args) - 1,))]
        + [pltpu.VMEM((8, d), F32), pltpu.VMEM((n - 1, 8, d), F32)]
        + [dma((2,)), dma((2, 4)), dma, dma]
        + [
            pltpu.VMEM((7, 4, quart, d), F32), pltpu.VMEM((7, 3, quart, d), F32),
            pltpu.VMEM((7, quart, d), F32), pltpu.VMEM((7, teams - 1, quart, d), F32),
        ]
        + [dma, dma((7,)), dma, dma((7,)), dma, dma],
        compiler_params=pltpu.CompilerParams(
            collective_id=0, has_side_effects=True, vmem_limit_bytes=60 << 20
        ),
    )(*args)
    outs = pl.pallas_call(
        deliver,
        out_shape=tuple(shape(out.shape, out.dtype) for out in outs),
        in_specs=[vmem] * len(outs),
        out_specs=(raw,) * len(outs),
        scratch_shapes=[dma((len(outs),))],
        compiler_params=pltpu.CompilerParams(vmem_limit_bytes=8 << 20),
    )(*outs)
    flat = lambda v: v.reshape(-1)
    return (
        outs[0], outs[1], outs[2], flat(outs[3]), outs[4], flat(outs[5]),
        outs[6], flat(outs[7]), outs[8], flat(outs[9]),
    )


def solution(mesh):
    global _axis_order
    _axis_order = tuple(mesh.axis_names)
    both = P(("rep", "dom"))
    both2 = P(("rep", "dom"), None)
    in_specs = (
        (both2,) * 4 + (P(),) * 8 + (both, P(("rep", "dom"), None, None), both2, both)
    )
    out_specs = (both2, both2) + (P("rep", None), P("rep")) * 4
    return jax.shard_map(body, mesh=mesh, in_specs=in_specs, out_specs=out_specs, check_vma=False)
```

```python
import functools
import math

import jax
import jax.numpy as jnp
from jax import lax
from jax.experimental import pallas as pl
from jax.experimental.pallas import tpu as pltpu
from jax.sharding import PartitionSpec as P

NPE = 512
LANES = 128
F32 = jnp.float32
BF16 = jnp.bfloat16
MESH = pl.DeviceIdType.MESH
CHUNK = 448


def divisor_up_to(total, cap):
    best = 16
    for size in range(16, cap + 1, 16):
        if total % size == 0:
            best = size
    return best


def mm(left, right):
    return lax.dot_general(left, right, (((1,), (0,)), ((), ())), preferred_element_type=F32)


def half_of(rows):
    return rows // 32 * 16


def in_two(step, left, right):
    cut = half_of(left.shape[0])
    return jnp.concatenate([step(left[:cut, :], right), step(left[cut:, :], right)], axis=0)


def mm2(left, right):
    return in_two(mm, left, right)


def mm_rt2(left, right):
    return in_two(mm_rt, left, right)


def mm_lt2(left, right):
    cut = half_of(left.shape[0])
    return mm_lt(left[:cut, :], right[:cut, :]) + mm_lt(left[cut:, :], right[cut:, :])


def mm_rt(left, right):
    return lax.dot_general(left, right, (((1,), (1,)), ((), ())), preferred_element_type=F32)


def mm_lt(left, right):
    return lax.dot_general(left, right, (((0,), (0,)), ((), ())), preferred_element_type=F32)


def halves(value):
    high = value.astype(BF16)
    low = (value - high.astype(F32)).astype(BF16)
    return high, low


def columns_of(row):
    return jnp.transpose(jnp.broadcast_to(row, (LANES, row.shape[1])))


def hits(ids, width, shift=0):
    lane = lax.broadcasted_iota(jnp.int32, ids.shape, 1).astype(F32)
    moved = ids + float(shift) if shift else ids
    tiles = [
        jnp.where(moved == lane + float(LANES * t + shift), 1.0, 0.0).astype(BF16)
        for t in range(width // LANES)
    ]
    return jnp.concatenate(tiles, axis=1)


def row_hits(row, height, shift=0):
    node = (lax.broadcasted_iota(jnp.int32, (height, row.shape[1]), 0) + shift).astype(F32)
    return jnp.where(row + float(shift) == node, 1.0, 0.0).astype(BF16)


def repeated(weight, times):
    rows, cols = weight.shape
    zero = jnp.zeros((rows, cols), weight.dtype)
    return jnp.concatenate(
        [
            jnp.concatenate([weight if a == b else zero for b in range(times)], axis=1)
            for a in range(times)
        ],
        axis=0,
    )


def activation(linear):
    squashed = 0.5 * jnp.tanh(0.5 * linear) + 0.5
    return linear * squashed, squashed * (1.0 + linear * (1.0 - squashed))


def fused(
    n, quarter, edge_scale, node_scale,
    nf_any, ef_any, nc_any, ec_any, wi_any, bi_any, wo_any, bo_any, wn_any, bn_any, wq_any,
    ends_any, live_any, lists_any, counts_any, mult_any,
    ng_ref, eg_ref, gwi_ref, gbi_ref, gwo_ref, gbo_ref, gwn_ref, gbn_ref, gwq_ref, gbq_ref,
    col_s, col_t, lcol, rows_s, deg_s, src_s, tgt_s, hid_s, slope_s, lin_s, giv_s, join_t, eb_s,
    sum_s, sum_t, pick_t, gwo_s, cot_s, hback_s, early_s, base_s, inv_s, agg_s,
    out1, in1, out2, in2,
    nf_ref, ef_ref, nc_ref, ec_ref, wi_ref, bi_ref, wo_ref, bo_ref, wn_ref, bn_ref, wq_ref,
    ends_ref, lists_ref, counts_ref, mult_ref, in_sem, bias_s, bias_l,
    px_send, px_recv, bs_send, bs_recv,
    qparts, qlands, mids, clands, qs_send, qs_recv, cs_send, cs_recv, gs_send, gs_recv,
):
    nodes = nf_ref.shape[0]
    d = nf_ref.shape[1]
    slots = nodes // NPE
    wide = slots * d
    edges = ends_ref.shape[1]
    me = lax.axis_index("dom")
    rep = lax.axis_index("rep")
    offsets = (1, -1, quarter, -quarter)
    order = _axis_order
    ch = divisor_up_to(edges, CHUNK)
    n_ch = edges // ch

    def device(index):
        return tuple(index if name == "dom" else rep for name in order)

    team, seat = me // 4, lax.rem(me, 4)
    teams = n // 4
    groups = (
        ((ends_any, ends_ref),),
        ((nf_any, nf_ref), (wi_any, wi_ref), (bi_any, bi_ref), (ef_any, ef_ref)),
        ((lists_any, lists_ref), (counts_any, counts_ref)),
        ((wo_any, wo_ref), (bo_any, bo_ref)),
        (
            (mult_any, mult_ref), (wq_any, wq_ref), (wn_any, wn_ref), (bn_any, bn_ref),
            (nc_any, nc_ref), (ec_any, ec_ref),
        ),
    )
    loads = []
    count = 0
    for group in groups:
        loads.append([])
        for source, target in group:
            loads[-1].append(pltpu.make_async_copy(source, target, in_sem.at[count]))
            loads[-1][-1].start()
            count += 1

    def arrive(which):
        for load in loads[which]:
            load.wait()

    barrier = pltpu.get_barrier_semaphore()

    def greet(i, carry):
        pl.semaphore_signal(
            barrier, inc=1, device_id=device(lax.rem(me + i, n)), device_id_type=MESH
        )
        return carry

    lax.fori_loop(1, n, greet, 0)

    arrive(0)
    ends = ends_ref[...].astype(F32)
    source_row, target_row = ends[0:1, :], ends[1:2, :]
    for start in range(0, edges, LANES):
        stop = min(start + LANES, edges)
        col_t[start:stop, :] = columns_of(ends[1:2, start:stop])
        col_s[start:stop, :] = columns_of(ends[0:1, start:stop])
    arrive(1)
    wi = wi_ref[...]
    ws, wt, we = wi[:d, :], wi[d : 2 * d, :], wi[2 * d :, :]
    by_slot = lambda v: jnp.concatenate(
        [v[e * NPE : (e + 1) * NPE, :] for e in range(slots)], axis=1
    )
    by_row = lambda v: jnp.concatenate(
        [v[:, e * d : (e + 1) * d] for e in range(slots)], axis=0
    )
    fold = lambda v: v[:, :d] + v[:, d:]
    pair_of = lambda v: jnp.concatenate(halves(v), axis=1)
    across = lambda ref, first, count, step: jnp.concatenate(
        [ref[e * step + first : e * step + first + count, :] for e in range(slots)], axis=1
    )
    twice = lambda v: jnp.concatenate([v] * slots, axis=1)
    nf2 = by_slot(nf_ref[...])
    w_in = jnp.concatenate([repeated(w, slots) for w in (ws, wt, we)], axis=0)
    bi_wide = twice(bi_ref[...])

    fwd = divisor_up_to(edges, 672)
    n_fwd = edges // fwd
    for c in range(n_fwd):
        rows = slice(c * fwd, (c + 1) * fwd)
        target = mm(hits(col_t[rows, :], NPE), nf2).astype(BF16)
        source = mm(hits(col_s[rows, :], NPE), nf2).astype(BF16)
        src_s[rows, :] = source
        tgt_s[rows, :] = target
        joined = jnp.concatenate([source, target, across(ef_ref, c * fwd, fwd, edges)], axis=1)
        hidden, slope = activation(mm2(joined, w_in) + bi_wide)
        hid_s[rows, :] = hidden.astype(BF16)
        slope_s[rows, :] = slope

    arrive(2)
    s_count = lists_ref.shape[1]
    lane_row = lax.broadcasted_iota(jnp.int32, (1, s_count), 1)
    for k in range(4):
        row = jnp.where(
            lane_row < counts_ref[:, k : k + 1], lists_ref[k : k + 1, :], -1
        ).astype(F32)
        rows_s[k] = jnp.broadcast_to(row, (8, s_count))
        lcol[k * s_count : (k + 1) * s_count, :] = columns_of(row)
    arrive(3)
    wo = wo_ref[...]
    wo_wide = repeated(wo, slots)
    nb = 128
    for b in range(NPE // nb):
        node_id = (lax.broadcasted_iota(jnp.int32, (nb, edges), 0) + b * nb).astype(F32)
        deg_s[b * nb : (b + 1) * nb, :] = jnp.broadcast_to(
            jnp.sum(jnp.where(target_row == node_id, 1.0, 0.0), axis=1, keepdims=True), (nb, d)
        )
    sums = mm(
        row_hits(target_row, NPE),
        jnp.concatenate([across(ef_ref, 0, edges, edges), hid_s[...]], axis=1),
    )
    sum_s[...] = sums[:, wide:]
    agg2 = (
        sums[:, :wide]
        + mm2(pair_of(sums[:, wide:]), jnp.concatenate([wo_wide, wo_wide], axis=0))
        + twice(deg_s[...] * bo_ref[...])
    )
    agg_s[...] = by_row(agg2)

    upper = me >= n // 2
    turns = [jnp.where(upper, a, b) for a, b in ((2, 3), (0, 1), (3, 2), (1, 0))]
    steps = [jnp.where(upper, offsets[a], offsets[b]) for a, b in ((2, 3), (0, 1), (3, 2), (1, 0))]

    def partner_copy(out, incoming, which, j):
        k = turns[j]
        other = k + 1 - 2 * lax.rem(k, 2)
        return pltpu.make_async_remote_copy(
            src_ref=out.at[k],
            dst_ref=incoming.at[other],
            send_sem=px_send.at[which],
            recv_sem=px_recv.at[which, other],
            device_id=device(lax.rem(me + steps[j] + n, n)),
            device_id_type=MESH,
        )

    def landing(out, incoming, which, j):
        k = turns[j]
        return pltpu.make_async_remote_copy(
            src_ref=out.at[k],
            dst_ref=incoming.at[k],
            send_sem=px_send.at[which],
            recv_sem=px_recv.at[which, k],
            device_id=device(lax.rem(me + 1, n)),
            device_id_type=MESH,
        )

    def send_shared(values, out, incoming, which):
        pair = pair_of(values)
        for k in range(4):
            out[k] = fold(
                mm(hits(lcol[k * s_count : (k + 1) * s_count, :], nodes, which), pair)
            )
        for j in range(4):
            partner_copy(out, incoming, which, j).start()

    def landed(out, incoming, which, js):
        for j in js:
            landing(out, incoming, which, j).wait_recv()
        moved = jnp.concatenate([incoming[turns[j]] for j in js], axis=0)
        entries = jnp.concatenate([rows_s[turns[j]][0:1, :] for j in js], axis=1)
        return pair_of(moved), entries

    near, far = (2, 3), (0, 1)
    pl.semaphore_wait(barrier, n - 1)
    send_shared(agg_s[...], out1, in1, 0)

    arrive(4)
    mult = mult_ref[...].astype(F32)
    for b in range(nodes // LANES):
        inv_s[b * LANES : (b + 1) * LANES, :] = 1.0 / columns_of(mult[b : b + 1, :])
    live = live_any[0]
    slot_of = lax.broadcasted_iota(jnp.int32, (nodes, d), 0) // NPE
    node_cot = jnp.where(slot_of < live, nc_ref[...].astype(F32), 0.0)
    cot_s[...] = node_cot.astype(BF16)
    wn = wn_ref[...]
    wn_wide = repeated(wn[d:, :], slots)
    hback_s[...] = mm_rt2(by_slot(cot_s[...]), repeated(wq_ref[...], slots))
    early_s[...] = mm2(nf2, repeated(wn[:d, :], slots)) + twice(bn_ref[...])
    bias_s[...] = jnp.zeros_like(bias_s)
    bias_s[3:4, :] = jnp.sum(node_cot, axis=0, keepdims=True)

    given_sum = jnp.zeros((1, d), F32)
    gwo = jnp.zeros((d, d), F32)
    for e in range(slots):
        lanes = slice(e * d, (e + 1) * d)
        given = jnp.where(
            jnp.broadcast_to(live, (edges, d)) > e,
            ec_ref[e * edges : (e + 1) * edges, :].astype(F32),
            0.0,
        )
        given_sum = given_sum + jnp.sum(given, axis=0, keepdims=True)
        giv_s[:, lanes] = given.astype(BF16)
        gwo = gwo + mm_lt(hid_s[:, lanes], giv_s[:, lanes])
    gwo_s[...] = gwo
    lin_s[...] = mm_rt2(giv_s[...], wo_wide)
    for at, block in enumerate((src_s[...], tgt_s[...], across(ef_ref, 0, edges, edges))):
        join_t[at * wide : (at + 1) * wide, :] = jnp.transpose(block)
    sum_rows = pair_of(by_row(sum_s[...]))
    picked = fold(mm2(hits(lcol[...], nodes, 2), sum_rows))
    pick_t[...] = jnp.transpose(pair_of(picked))
    sum_t[...] = jnp.transpose(sum_rows)

    def gather_in(js):
        moved, entries = landed(out1, in1, 0, js)
        return agg_s[...] + fold(mm2(row_hits(entries, nodes), moved))

    agg_s[...] = gather_in(near)
    consistent = (gather_in(far) * inv_s[...]).astype(BF16)
    node_hidden, node_slope = activation(early_s[...] + mm2(by_slot(consistent), wn_wide))
    node_back2 = (hback_s[...] * node_slope).astype(BF16)
    back = by_row(mm_rt2(node_back2, wn_wide)) * inv_s[...]
    agg_s[...] = back
    send_shared(back, out2, in2, 1)

    quart = qparts.shape[2]
    results = (
        (gwn_ref, 0, node_scale), (gwn_ref, d, node_scale), (gwq_ref, 0, node_scale),
        (gwo_ref, 0, edge_scale),
        (gwi_ref, 2 * d, edge_scale), (gwi_ref, d, edge_scale), (gwi_ref, 0, edge_scale),
    )

    def seat_of(i):
        return lax.rem(seat + i, 4)

    def split_copy(p, i):
        return pltpu.make_async_remote_copy(
            src_ref=qparts.at[p, seat_of(i)],
            dst_ref=qlands.at[p, i - 1],
            send_sem=qs_send,
            recv_sem=qs_recv.at[p],
            device_id=device(4 * team + seat_of(i)),
            device_id_type=MESH,
        )

    def cross_copy(p, i):
        return pltpu.make_async_remote_copy(
            src_ref=mids.at[p],
            dst_ref=clands.at[p, i - 1],
            send_sem=cs_send,
            recv_sem=cs_recv.at[p],
            device_id=device(4 * lax.rem(team + i, teams) + seat),
            device_id_type=MESH,
        )

    def share_copy(p, i):
        ref, first, _ = results[p]
        rows = pl.ds(pl.multiple_of(first + seat * quart, 8), quart)
        return pltpu.make_async_remote_copy(
            src_ref=ref.at[rows],
            dst_ref=ref.at[rows],
            send_sem=gs_send,
            recv_sem=gs_recv,
            device_id=device(4 * team + seat_of(i)),
            device_id_type=MESH,
        )

    def whole(ref, send_sem, recv_sem):
        return pltpu.make_async_remote_copy(
            src_ref=ref,
            dst_ref=ref,
            send_sem=send_sem,
            recv_sem=recv_sem,
            device_id=device(lax.rem(me + 1, n)),
            device_id_type=MESH,
        )

    def hold(p, value):
        for j in range(4):
            qparts[p, j] = value[j * quart : (j + 1) * quart, :]

    def push(p):
        for i in (2, 1, 3):
            split_copy(p, i).start()

    def cross(p):
        whole(qlands.at[p], qs_send, qs_recv.at[p]).wait_recv()
        total = qparts[p, seat]
        for i in range(3):
            total = total + qlands[p, i]
        mids[p] = total
        for i in range(1, teams):
            cross_copy(p, i).start()

    def share(p):
        whole(clands.at[p], cs_send, cs_recv.at[p]).wait_recv()
        total = mids[p]
        for i in range(teams - 1):
            total = total + clands[p, i]
        ref, first, scale = results[p]
        ref[pl.ds(pl.multiple_of(first + seat * quart, 8), quart), :] = total * scale
        for i in (2, 1, 3):
            share_copy(p, i).start()

    node_back = by_row(node_back2)
    hold(0, mm_lt2(nf_ref[...], node_back))
    hold(1, mm_lt2(consistent, node_back))
    hold(2, mm_lt2(by_row(node_hidden.astype(BF16)), cot_s[...]))
    bias_s[2:3, :] = jnp.sum(node_back.astype(F32), axis=0, keepdims=True)
    base_s[...] = cot_s[...].astype(F32) + mm_rt2(node_back, wn[:d, :])
    wo_rows = jnp.concatenate([wo, wo], axis=1)
    pair_back = pair_of(back)
    crossed = mm2(sum_t[...], pair_back)
    gwo_s[...] = gwo_s[...] + fold(crossed[:d, :]) + fold(crossed[d:, :])
    spread_back = by_slot(mm_rt2(pair_back, wo_rows))
    for c in range(n_ch):
        rows = slice(c * ch, (c + 1) * ch)
        got = mm(hits(col_t[rows, :], NPE, 1), pair_of(spread_back))
        lin_s[rows, :] = lin_s[rows, :] + got[:, :wide] + got[:, wide:]

    for p in range(3):
        push(p)

    def toward(moved, entries, e):
        wanted = entries - float(NPE * e)
        marks = jnp.concatenate(
            [
                jnp.where(col_t[...] == wanted[:, t * LANES : (t + 1) * LANES], 1.0, 0.0).astype(BF16)
                for t in range(entries.shape[1] // LANES)
            ],
            axis=1,
        )
        return fold(mm(marks, moved))

    moved, entries = landed(out2, in2, 1, near)
    moved = pair_of(mm_rt2(moved, wo_rows))
    for e in range(slots):
        lanes = slice(e * d, (e + 1) * d)
        lin_s[:, lanes] = lin_s[:, lanes] + toward(moved, entries, e)
    moved, entries = landed(out2, in2, 1, far)
    moved = pair_of(mm_rt2(moved, wo_rows))
    for e in range(slots):
        lanes = slice(e * d, (e + 1) * d)
        eb_s[:, lanes] = (
            (lin_s[:, lanes] + toward(moved, entries, e)) * slope_s[:, lanes]
        ).astype(BF16)
    arrived = pair_of(jnp.concatenate([in2[k] for k in range(4)], axis=0))
    added = mm2(pick_t[...], arrived)
    hold(3, gwo_s[...] + fold(added[:d, :]) + fold(added[d:, :]))
    push(3)

    def weigh(at):
        total = None
        for e in range(slots):
            first = at * wide + e * d
            both = mm(join_t[first : first + d, :], eb_s[...])[:, e * d : (e + 1) * d]
            total = both if total is None else total + both
        return total

    for at in (2, 1, 0):
        hold(6 - at, weigh(at))
        push(6 - at)
    for p in range(0, 3):
        cross(p)
    column = jnp.sum(eb_s[...].astype(F32), axis=0, keepdims=True)
    bias_row = column[:, :d]
    for e in range(1, slots):
        bias_row = bias_row + column[:, e * d : (e + 1) * d]
    bias_s[0:1, :] = bias_row
    entry_row = jnp.concatenate([rows_s[k][0:1, :] for k in range(4)], axis=1)
    agg_back = agg_s[...] + fold(mm2(row_hits(entry_row, nodes, 1), arrived))
    degrees = jnp.concatenate([deg_s[...]] * slots, axis=0)
    bias_s[1:2, :] = given_sum + jnp.sum(degrees * agg_back, axis=0, keepdims=True)

    def bias_copy(i):
        return pltpu.make_async_remote_copy(
            src_ref=bias_s,
            dst_ref=bias_l.at[i - 1],
            send_sem=bs_send,
            recv_sem=bs_recv,
            device_id=device(lax.rem(me + i, n)),
            device_id_type=MESH,
        )

    lax.fori_loop(1, n, lambda i, x: (bias_copy(i).start(), x)[1], 0)

    eb2 = eb_s[...]
    we_wide = repeated(we, slots)
    quad = pair_of(by_slot(agg_back))
    for c in range(n_ch):
        rows = slice(c * ch, (c + 1) * ch)
        got = mm(hits(col_t[rows, :], NPE, 2), quad)
        cot = giv_s[rows, :].astype(F32) + (got[:, :wide] + got[:, wide:])
        value = (cot + mm_rt(eb_s[rows, :], we_wide)).astype(BF16)
        for e in range(slots):
            eg_ref[e * edges + c * ch : e * edges + (c + 1) * ch, :] = value[
                :, e * d : (e + 1) * d
            ]
    cross(3)
    by_target = pair_of(by_row(mm2(row_hits(target_row, NPE, 1), eb2)))
    for p in range(4, 7):
        cross(p)
    for p in range(0, 3):
        share(p)
    by_source = pair_of(by_row(mm2(row_hits(source_row, NPE, 1), eb2)))
    w4 = jnp.concatenate([ws, ws, wt, wt], axis=1)
    spread = jnp.concatenate([by_source, by_target], axis=1)
    ng_ref[...] = (base_s[...] + mm_rt2(spread, w4)).astype(BF16)
    for p in range(3, 7):
        share(p)

    whole(bias_l, bs_send, bs_recv).wait_recv()
    bias = lax.fori_loop(1, n, lambda i, total: total + bias_l[i - 1], bias_s[...])
    gbi_ref[...] = bias[0:1, :] * edge_scale
    gbo_ref[...] = bias[1:2, :] * edge_scale
    gbn_ref[...] = bias[2:3, :] * node_scale
    gbq_ref[...] = bias[3:4, :] * node_scale
    whole(bias_l, bs_send, bs_recv).wait_send()
    whole(in1, px_send.at[0], px_recv.at[0, 0]).wait_send()
    whole(in2, px_send.at[1], px_recv.at[1, 0]).wait_send()
    whole(qlands, qs_send, qs_recv.at[0]).wait_send()
    whole(clands, cs_send, cs_recv.at[0]).wait_send()
    whole(qlands, gs_send, gs_recv).wait()


def deliver(*refs):
    count = len(refs) // 2
    sems = refs[-1]
    copies = [
        pltpu.make_async_copy(refs[i], refs[count + i], sems.at[i]) for i in range(count)
    ]
    for copy in copies:
        copy.start()
    for copy in copies:
        copy.wait()


_axis_order = ("dom", "rep")


def body(
    node_features, edge_features, node_cotangent, edge_cotangent,
    edge_in_weight, edge_in_bias, edge_out_weight, edge_out_bias,
    node_in_weight, node_in_bias, node_out_weight,
    edge_ends, live_elements, shared_nodes, shared_counts, multiplicity,
):
    n = lax.axis_size("dom")
    nodes, d = node_features.shape
    rows = edge_features.shape[0]
    edges = edge_ends.shape[1]
    s_count = shared_nodes.shape[2]
    hid = edge_in_weight.shape[1]
    edge_scale = 1.0 / math.sqrt(rows * n)
    node_scale = 1.0 / math.sqrt(nodes * n)
    slots = nodes // NPE
    quart = d // 4
    teams = n // 4
    vmem = pl.BlockSpec(memory_space=pltpu.VMEM)
    raw = pl.BlockSpec(memory_space=pl.ANY)
    hbm = pl.BlockSpec(memory_space=pltpu.HBM)
    shape = jax.ShapeDtypeStruct
    dma = pltpu.SemaphoreType.DMA
    vshape = pltpu.VMEM
    row = vshape((1, d), F32)
    args = (
        node_features, edge_features, node_cotangent, edge_cotangent,
        edge_in_weight, edge_in_bias.reshape(1, -1), edge_out_weight, edge_out_bias.reshape(1, -1),
        node_in_weight, node_in_bias.reshape(1, -1), node_out_weight,
        edge_ends, live_elements, shared_nodes[0], shared_counts,
        multiplicity.reshape(-1, LANES),
    )

    outs = pl.pallas_call(
        functools.partial(fused, n, n // 4, edge_scale, node_scale),
        out_shape=(
            vshape((nodes, d), BF16), vshape((rows, d), BF16),
            vshape((3 * d, hid), F32), row, vshape((hid, d), F32), row,
            vshape((2 * d, hid), F32), row, vshape((hid, d), F32), row,
        ),
        in_specs=[hbm] * 12 + [pl.BlockSpec(memory_space=pltpu.SMEM)] + [hbm] * 3,
        out_specs=(vmem,) * 10,
        scratch_shapes=[
            pltpu.VMEM((edges, LANES), F32), pltpu.VMEM((edges, LANES), F32),
            pltpu.VMEM((4 * s_count, LANES), F32), pltpu.VMEM((4, 8, s_count), F32),
            pltpu.VMEM((NPE, d), F32),
            pltpu.VMEM((edges, slots * d), BF16), pltpu.VMEM((edges, slots * d), BF16),
            pltpu.VMEM((edges, slots * hid), BF16), pltpu.VMEM((edges, slots * hid), F32),
            pltpu.VMEM((edges, slots * hid), F32), pltpu.VMEM((edges, slots * d), BF16),
            pltpu.VMEM((3 * slots * d, edges), BF16), pltpu.VMEM((edges, slots * hid), BF16),
            pltpu.VMEM((NPE, slots * hid), F32), pltpu.VMEM((2 * hid, nodes), BF16),
            pltpu.VMEM((2 * hid, 4 * s_count), BF16), pltpu.VMEM((hid, d), F32),
            pltpu.VMEM((nodes, d), BF16), pltpu.VMEM((NPE, slots * hid), F32),
            pltpu.VMEM((NPE, slots * hid), F32), pltpu.VMEM((nodes, d), F32),
            pltpu.VMEM((nodes, d), F32), pltpu.VMEM((nodes, d), F32),
        ]
        + [pltpu.VMEM((4, s_count, d), F32)] * 4
        + [pltpu.VMEM(arg.shape, arg.dtype) for i, arg in enumerate(args) if i != 12]
        + [dma((len(args) - 1,))]
        + [pltpu.VMEM((8, d), F32), pltpu.VMEM((n - 1, 8, d), F32)]
        + [dma((2,)), dma((2, 4)), dma, dma]
        + [
            pltpu.VMEM((7, 4, quart, d), F32), pltpu.VMEM((7, 3, quart, d), F32),
            pltpu.VMEM((7, quart, d), F32), pltpu.VMEM((7, teams - 1, quart, d), F32),
        ]
        + [dma, dma((7,)), dma, dma((7,)), dma, dma],
        compiler_params=pltpu.CompilerParams(
            collective_id=0, has_side_effects=True, vmem_limit_bytes=60 << 20
        ),
    )(*args)
    outs = pl.pallas_call(
        deliver,
        out_shape=tuple(shape(out.shape, out.dtype) for out in outs),
        in_specs=[vmem] * len(outs),
        out_specs=(raw,) * len(outs),
        scratch_shapes=[dma((len(outs),))],
        compiler_params=pltpu.CompilerParams(vmem_limit_bytes=8 << 20),
    )(*outs)
    flat = lambda v: v.reshape(-1)
    return (
        outs[0], outs[1], outs[2], flat(outs[3]), outs[4], flat(outs[5]),
        outs[6], flat(outs[7]), outs[8], flat(outs[9]),
    )


def solution(mesh):
    global _axis_order
    _axis_order = tuple(mesh.axis_names)
    both = P(("rep", "dom"))
    both2 = P(("rep", "dom"), None)
    in_specs = (
        (both2,) * 4 + (P(),) * 8 + (both, P(("rep", "dom"), None, None), both2, both)
    )
    out_specs = (both2, both2) + (P("rep", None), P("rep")) * 4
    return jax.shard_map(body, mesh=mesh, in_specs=in_specs, out_specs=out_specs, check_vma=False)
```

```python
import functools
import math

import jax
import jax.numpy as jnp
from jax import lax
from jax.experimental import pallas as pl
from jax.experimental.pallas import tpu as pltpu
from jax.sharding import PartitionSpec as P

NPE = 512
LANES = 128
F32 = jnp.float32
BF16 = jnp.bfloat16
MESH = pl.DeviceIdType.MESH
CHUNK = 448


def divisor_up_to(total, cap):
    best = 16
    for size in range(16, cap + 1, 16):
        if total % size == 0:
            best = size
    return best


def mm(left, right):
    return lax.dot_general(left, right, (((1,), (0,)), ((), ())), preferred_element_type=F32)


def half_of(rows):
    return rows // 32 * 16


def in_two(step, left, right):
    cut = half_of(left.shape[0])
    return jnp.concatenate([step(left[:cut, :], right), step(left[cut:, :], right)], axis=0)


def mm2(left, right):
    return in_two(mm, left, right)


def mm_rt2(left, right):
    return in_two(mm_rt, left, right)


def mm_lt2(left, right):
    cut = half_of(left.shape[0])
    return mm_lt(left[:cut, :], right[:cut, :]) + mm_lt(left[cut:, :], right[cut:, :])


def mm_rt(left, right):
    return lax.dot_general(left, right, (((1,), (1,)), ((), ())), preferred_element_type=F32)


def mm_lt(left, right):
    return lax.dot_general(left, right, (((0,), (0,)), ((), ())), preferred_element_type=F32)


def halves(value):
    high = value.astype(BF16)
    low = (value - high.astype(F32)).astype(BF16)
    return high, low


def columns_of(row):
    return jnp.transpose(jnp.broadcast_to(row, (LANES, row.shape[1])))


def hits(ids, width, shift=0):
    lane = lax.broadcasted_iota(jnp.int32, ids.shape, 1).astype(F32)
    moved = ids + float(shift) if shift else ids
    tiles = [
        jnp.where(moved == lane + float(LANES * t + shift), 1.0, 0.0).astype(BF16)
        for t in range(width // LANES)
    ]
    return jnp.concatenate(tiles, axis=1)


def row_hits(row, height, shift=0):
    node = (lax.broadcasted_iota(jnp.int32, (height, row.shape[1]), 0) + shift).astype(F32)
    return jnp.where(row + float(shift) == node, 1.0, 0.0).astype(BF16)


def repeated(weight, times):
    rows, cols = weight.shape
    zero = jnp.zeros((rows, cols), weight.dtype)
    return jnp.concatenate(
        [
            jnp.concatenate([weight if a == b else zero for b in range(times)], axis=1)
            for a in range(times)
        ],
        axis=0,
    )


def activation(linear):
    squashed = 0.5 * jnp.tanh(0.5 * linear) + 0.5
    return linear * squashed, squashed * (1.0 + linear * (1.0 - squashed))


def fused(
    n, quarter, edge_scale, node_scale,
    nf_any, ef_any, nc_any, ec_any, wi_any, bi_any, wo_any, bo_any, wn_any, bn_any, wq_any,
    ends_any, live_any, lists_any, counts_any, mult_any,
    ng_ref, eg_ref, gwi_ref, gbi_ref, gwo_ref, gbo_ref, gwn_ref, gbn_ref, gwq_ref, gbq_ref,
    col_s, col_t, lcol, rows_s, deg_s, src_s, tgt_s, hid_s, slope_s, lin_s, giv_s, join_t, eb_s,
    sum_s, sum_t, pick_t, gwo_s, cot_s, hback_s, early_s, base_s, inv_s, agg_s,
    out1, in1, out2, in2,
    nf_ref, ef_ref, nc_ref, ec_ref, wi_ref, bi_ref, wo_ref, bo_ref, wn_ref, bn_ref, wq_ref,
    ends_ref, lists_ref, counts_ref, mult_ref, in_sem, bias_s, bias_l,
    px_send, px_recv, bs_send, bs_recv,
    qparts, qlands, mids, clands, qs_send, qs_recv, cs_send, cs_recv, gs_send, gs_recv,
):
    nodes = nf_ref.shape[0]
    d = nf_ref.shape[1]
    slots = nodes // NPE
    wide = slots * d
    edges = ends_ref.shape[1]
    me = lax.axis_index("dom")
    rep = lax.axis_index("rep")
    offsets = (1, -1, quarter, -quarter)
    order = _axis_order
    ch = divisor_up_to(edges, CHUNK)
    n_ch = edges // ch

    def device(index):
        return tuple(index if name == "dom" else rep for name in order)

    team, seat = me // 4, lax.rem(me, 4)
    teams = n // 4
    groups = (
        ((ends_any, ends_ref),),
        ((nf_any, nf_ref), (wi_any, wi_ref), (bi_any, bi_ref), (ef_any, ef_ref)),
        ((lists_any, lists_ref), (counts_any, counts_ref)),
        ((wo_any, wo_ref), (bo_any, bo_ref)),
        (
            (mult_any, mult_ref), (wq_any, wq_ref), (wn_any, wn_ref), (bn_any, bn_ref),
            (nc_any, nc_ref), (ec_any, ec_ref),
        ),
    )
    loads = []
    count = 0
    for group in groups:
        loads.append([])
        for source, target in group:
            loads[-1].append(pltpu.make_async_copy(source, target, in_sem.at[count]))
            loads[-1][-1].start()
            count += 1

    def arrive(which):
        for load in loads[which]:
            load.wait()

    barrier = pltpu.get_barrier_semaphore()

    def greet(i, carry):
        pl.semaphore_signal(
            barrier, inc=1, device_id=device(lax.rem(me + i, n)), device_id_type=MESH
        )
        return carry

    lax.fori_loop(1, n, greet, 0)

    arrive(0)
    ends = ends_ref[...].astype(F32)
    source_row, target_row = ends[0:1, :], ends[1:2, :]
    for start in range(0, edges, LANES):
        stop = min(start + LANES, edges)
        col_t[start:stop, :] = columns_of(ends[1:2, start:stop])
        col_s[start:stop, :] = columns_of(ends[0:1, start:stop])
    arrive(1)
    wi = wi_ref[...]
    ws, wt, we = wi[:d, :], wi[d : 2 * d, :], wi[2 * d :, :]
    by_slot = lambda v: jnp.concatenate(
        [v[e * NPE : (e + 1) * NPE, :] for e in range(slots)], axis=1
    )
    by_row = lambda v: jnp.concatenate(
        [v[:, e * d : (e + 1) * d] for e in range(slots)], axis=0
    )
    fold = lambda v: v[:, :d] + v[:, d:]
    pair_of = lambda v: jnp.concatenate(halves(v), axis=1)
    across = lambda ref, first, count, step: jnp.concatenate(
        [ref[e * step + first : e * step + first + count, :] for e in range(slots)], axis=1
    )
    twice = lambda v: jnp.concatenate([v] * slots, axis=1)
    nf2 = by_slot(nf_ref[...])
    w_in = jnp.concatenate([repeated(w, slots) for w in (ws, wt, we)], axis=0)
    bi_wide = twice(bi_ref[...])

    fwd = divisor_up_to(edges, 672)
    n_fwd = edges // fwd
    for c in range(n_fwd):
        rows = slice(c * fwd, (c + 1) * fwd)
        target = mm(hits(col_t[rows, :], NPE), nf2).astype(BF16)
        source = mm(hits(col_s[rows, :], NPE), nf2).astype(BF16)
        src_s[rows, :] = source
        tgt_s[rows, :] = target
        joined = jnp.concatenate([source, target, across(ef_ref, c * fwd, fwd, edges)], axis=1)
        hidden, slope = activation(mm2(joined, w_in) + bi_wide)
        hid_s[rows, :] = hidden.astype(BF16)
        slope_s[rows, :] = slope

    arrive(2)
    s_count = lists_ref.shape[1]
    lane_row = lax.broadcasted_iota(jnp.int32, (1, s_count), 1)
    for k in range(4):
        row = jnp.where(
            lane_row < counts_ref[:, k : k + 1], lists_ref[k : k + 1, :], -1
        ).astype(F32)
        rows_s[k] = jnp.broadcast_to(row, (8, s_count))
        lcol[k * s_count : (k + 1) * s_count, :] = columns_of(row)
    arrive(3)
    wo = wo_ref[...]
    wo_wide = repeated(wo, slots)
    nb = 128
    for b in range(NPE // nb):
        node_id = (lax.broadcasted_iota(jnp.int32, (nb, edges), 0) + b * nb).astype(F32)
        deg_s[b * nb : (b + 1) * nb, :] = jnp.broadcast_to(
            jnp.sum(jnp.where(target_row == node_id, 1.0, 0.0), axis=1, keepdims=True), (nb, d)
        )
    sums = mm(
        row_hits(target_row, NPE),
        jnp.concatenate([across(ef_ref, 0, edges, edges), hid_s[...]], axis=1),
    )
    sum_s[...] = sums[:, wide:]
    agg2 = (
        sums[:, :wide]
        + mm2(pair_of(sums[:, wide:]), jnp.concatenate([wo_wide, wo_wide], axis=0))
        + twice(deg_s[...] * bo_ref[...])
    )
    agg_s[...] = by_row(agg2)

    upper = me >= n // 2
    turns = [jnp.where(upper, a, b) for a, b in ((2, 3), (0, 1), (3, 2), (1, 0))]
    steps = [jnp.where(upper, offsets[a], offsets[b]) for a, b in ((2, 3), (0, 1), (3, 2), (1, 0))]

    def partner_copy(out, incoming, which, j):
        k = turns[j]
        other = k + 1 - 2 * lax.rem(k, 2)
        return pltpu.make_async_remote_copy(
            src_ref=out.at[k],
            dst_ref=incoming.at[other],
            send_sem=px_send.at[which],
            recv_sem=px_recv.at[which, other],
            device_id=device(lax.rem(me + steps[j] + n, n)),
            device_id_type=MESH,
        )

    def landing(out, incoming, which, j):
        k = turns[j]
        return pltpu.make_async_remote_copy(
            src_ref=out.at[k],
            dst_ref=incoming.at[k],
            send_sem=px_send.at[which],
            recv_sem=px_recv.at[which, k],
            device_id=device(lax.rem(me + 1, n)),
            device_id_type=MESH,
        )

    def send_shared(values, out, incoming, which):
        pair = pair_of(values)
        for k in range(4):
            out[k] = fold(
                mm(hits(lcol[k * s_count : (k + 1) * s_count, :], nodes, which), pair)
            )
        for j in (0, 1, 3, 2):
            partner_copy(out, incoming, which, j).start()

    def landed(out, incoming, which, js):
        for j in js:
            landing(out, incoming, which, j).wait_recv()
        moved = jnp.concatenate([incoming[turns[j]] for j in js], axis=0)
        entries = jnp.concatenate([rows_s[turns[j]][0:1, :] for j in js], axis=1)
        return pair_of(moved), entries

    near, far = (2, 3), (0, 1)
    pl.semaphore_wait(barrier, n - 1)
    send_shared(agg_s[...], out1, in1, 0)

    arrive(4)
    mult = mult_ref[...].astype(F32)
    for b in range(nodes // LANES):
        inv_s[b * LANES : (b + 1) * LANES, :] = 1.0 / columns_of(mult[b : b + 1, :])
    live = live_any[0]
    slot_of = lax.broadcasted_iota(jnp.int32, (nodes, d), 0) // NPE
    node_cot = jnp.where(slot_of < live, nc_ref[...].astype(F32), 0.0)
    cot_s[...] = node_cot.astype(BF16)
    wn = wn_ref[...]
    wn_wide = repeated(wn[d:, :], slots)
    hback_s[...] = mm_rt2(by_slot(cot_s[...]), repeated(wq_ref[...], slots))
    early_s[...] = mm2(nf2, repeated(wn[:d, :], slots)) + twice(bn_ref[...])
    bias_s[...] = jnp.zeros_like(bias_s)
    bias_s[3:4, :] = jnp.sum(node_cot, axis=0, keepdims=True)

    given_sum = jnp.zeros((1, d), F32)
    gwo = jnp.zeros((d, d), F32)
    for e in range(slots):
        lanes = slice(e * d, (e + 1) * d)
        given = jnp.where(
            jnp.broadcast_to(live, (edges, d)) > e,
            ec_ref[e * edges : (e + 1) * edges, :].astype(F32),
            0.0,
        )
        given_sum = given_sum + jnp.sum(given, axis=0, keepdims=True)
        giv_s[:, lanes] = given.astype(BF16)
        gwo = gwo + mm_lt(hid_s[:, lanes], giv_s[:, lanes])
    gwo_s[...] = gwo
    lin_s[...] = mm_rt2(giv_s[...], wo_wide)
    for at, block in enumerate((src_s[...], tgt_s[...], across(ef_ref, 0, edges, edges))):
        join_t[at * wide : (at + 1) * wide, :] = jnp.transpose(block)
    sum_rows = pair_of(by_row(sum_s[...]))
    picked = fold(mm2(hits(lcol[...], nodes, 2), sum_rows))
    pick_t[...] = jnp.transpose(pair_of(picked))
    sum_t[...] = jnp.transpose(sum_rows)

    def gather_in(js):
        moved, entries = landed(out1, in1, 0, js)
        return agg_s[...] + fold(mm2(row_hits(entries, nodes), moved))

    agg_s[...] = gather_in(near)
    consistent = (gather_in(far) * inv_s[...]).astype(BF16)
    node_hidden, node_slope = activation(early_s[...] + mm2(by_slot(consistent), wn_wide))
    node_back2 = (hback_s[...] * node_slope).astype(BF16)
    back = by_row(mm_rt2(node_back2, wn_wide)) * inv_s[...]
    agg_s[...] = back
    send_shared(back, out2, in2, 1)

    quart = qparts.shape[2]
    results = (
        (gwn_ref, 0, node_scale), (gwn_ref, d, node_scale), (gwq_ref, 0, node_scale),
        (gwo_ref, 0, edge_scale),
        (gwi_ref, 2 * d, edge_scale), (gwi_ref, d, edge_scale), (gwi_ref, 0, edge_scale),
    )

    def seat_of(i):
        if i == 1:
            return seat + 1 - 2 * lax.rem(seat, 2)
        return lax.rem(seat + 2, 4) if i == 2 else 3 - seat

    def split_copy(p, i):
        return pltpu.make_async_remote_copy(
            src_ref=qparts.at[p, seat_of(i)],
            dst_ref=qlands.at[p, i - 1],
            send_sem=qs_send,
            recv_sem=qs_recv.at[p],
            device_id=device(4 * team + seat_of(i)),
            device_id_type=MESH,
        )

    def cross_copy(p, i):
        return pltpu.make_async_remote_copy(
            src_ref=mids.at[p],
            dst_ref=clands.at[p, i - 1],
            send_sem=cs_send,
            recv_sem=cs_recv.at[p],
            device_id=device(4 * lax.rem(team + i, teams) + seat),
            device_id_type=MESH,
        )

    def share_copy(p, i):
        ref, first, _ = results[p]
        rows = pl.ds(pl.multiple_of(first + seat * quart, 8), quart)
        return pltpu.make_async_remote_copy(
            src_ref=ref.at[rows],
            dst_ref=ref.at[rows],
            send_sem=gs_send,
            recv_sem=gs_recv,
            device_id=device(4 * team + seat_of(i)),
            device_id_type=MESH,
        )

    def whole(ref, send_sem, recv_sem):
        return pltpu.make_async_remote_copy(
            src_ref=ref,
            dst_ref=ref,
            send_sem=send_sem,
            recv_sem=recv_sem,
            device_id=device(lax.rem(me + 1, n)),
            device_id_type=MESH,
        )

    def hold(p, value):
        for j in range(4):
            qparts[p, j] = value[j * quart : (j + 1) * quart, :]

    def push(p):
        for i in (3, 2, 1):
            split_copy(p, i).start()

    def cross(p):
        whole(qlands.at[p], qs_send, qs_recv.at[p]).wait_recv()
        total = qparts[p, seat]
        for i in range(3):
            total = total + qlands[p, i]
        mids[p] = total
        for i in range(1, teams):
            cross_copy(p, i).start()

    def share(p):
        whole(clands.at[p], cs_send, cs_recv.at[p]).wait_recv()
        total = mids[p]
        for i in range(teams - 1):
            total = total + clands[p, i]
        ref, first, scale = results[p]
        ref[pl.ds(pl.multiple_of(first + seat * quart, 8), quart), :] = total * scale
        for i in (3, 2, 1):
            share_copy(p, i).start()

    node_back = by_row(node_back2)
    hold(0, mm_lt2(nf_ref[...], node_back))
    hold(1, mm_lt2(consistent, node_back))
    hold(2, mm_lt2(by_row(node_hidden.astype(BF16)), cot_s[...]))
    for p in range(3):
        push(p)
    bias_s[2:3, :] = jnp.sum(node_back.astype(F32), axis=0, keepdims=True)
    base_s[...] = cot_s[...].astype(F32) + mm_rt2(node_back, wn[:d, :])
    wo_rows = jnp.concatenate([wo, wo], axis=1)
    pair_back = pair_of(back)
    crossed = mm2(sum_t[...], pair_back)
    gwo_s[...] = gwo_s[...] + fold(crossed[:d, :]) + fold(crossed[d:, :])
    spread_back = by_slot(mm_rt2(pair_back, wo_rows))
    for c in range(n_ch):
        rows = slice(c * ch, (c + 1) * ch)
        got = mm(hits(col_t[rows, :], NPE, 1), pair_of(spread_back))
        lin_s[rows, :] = lin_s[rows, :] + got[:, :wide] + got[:, wide:]

    def toward(moved, entries, e):
        wanted = entries - float(NPE * e)
        marks = jnp.concatenate(
            [
                jnp.where(col_t[...] == wanted[:, t * LANES : (t + 1) * LANES], 1.0, 0.0).astype(BF16)
                for t in range(entries.shape[1] // LANES)
            ],
            axis=1,
        )
        return fold(mm2(marks, moved))

    moved, entries = landed(out2, in2, 1, near)
    moved = pair_of(mm_rt2(moved, wo_rows))
    for e in range(slots):
        lanes = slice(e * d, (e + 1) * d)
        lin_s[:, lanes] = lin_s[:, lanes] + toward(moved, entries, e)
    moved, entries = landed(out2, in2, 1, far)
    moved = pair_of(mm_rt2(moved, wo_rows))
    for e in range(slots):
        lanes = slice(e * d, (e + 1) * d)
        eb_s[:, lanes] = (
            (lin_s[:, lanes] + toward(moved, entries, e)) * slope_s[:, lanes]
        ).astype(BF16)
    arrived = pair_of(jnp.concatenate([in2[k] for k in range(4)], axis=0))
    added = mm2(pick_t[...], arrived)
    hold(3, gwo_s[...] + fold(added[:d, :]) + fold(added[d:, :]))
    push(3)

    def weigh(at):
        total = None
        for e in range(slots):
            first = at * wide + e * d
            both = mm(join_t[first : first + d, :], eb_s[...])[:, e * d : (e + 1) * d]
            total = both if total is None else total + both
        return total

    for at in (2, 1, 0):
        hold(6 - at, weigh(at))
        push(6 - at)
    for p in range(0, 3):
        cross(p)
    column = jnp.sum(eb_s[...].astype(F32), axis=0, keepdims=True)
    bias_row = column[:, :d]
    for e in range(1, slots):
        bias_row = bias_row + column[:, e * d : (e + 1) * d]
    bias_s[0:1, :] = bias_row
    entry_row = jnp.concatenate([rows_s[k][0:1, :] for k in range(4)], axis=1)
    agg_back = agg_s[...] + fold(mm2(row_hits(entry_row, nodes, 1), arrived))
    degrees = jnp.concatenate([deg_s[...]] * slots, axis=0)
    bias_s[1:2, :] = given_sum + jnp.sum(degrees * agg_back, axis=0, keepdims=True)

    def bias_copy(i):
        return pltpu.make_async_remote_copy(
            src_ref=bias_s,
            dst_ref=bias_l.at[i - 1],
            send_sem=bs_send,
            recv_sem=bs_recv,
            device_id=device(lax.rem(me + i, n)),
            device_id_type=MESH,
        )

    eb2 = eb_s[...]
    we_wide = repeated(we, slots)
    quad = pair_of(by_slot(agg_back))
    for c in range(n_ch):
        rows = slice(c * ch, (c + 1) * ch)
        got = mm(hits(col_t[rows, :], NPE, 2), quad)
        cot = giv_s[rows, :].astype(F32) + (got[:, :wide] + got[:, wide:])
        value = (cot + mm_rt(eb_s[rows, :], we_wide)).astype(BF16)
        for e in range(slots):
            eg_ref[e * edges + c * ch : e * edges + (c + 1) * ch, :] = value[
                :, e * d : (e + 1) * d
            ]
    cross(3)
    lax.fori_loop(1, n, lambda i, x: (bias_copy(i).start(), x)[1], 0)

    by_target = pair_of(by_row(mm2(row_hits(target_row, NPE, 1), eb2)))
    for p in range(4, 7):
        cross(p)
    for p in range(0, 3):
        share(p)
    by_source = pair_of(by_row(mm2(row_hits(source_row, NPE, 1), eb2)))
    w4 = jnp.concatenate([ws, ws, wt, wt], axis=1)
    spread = jnp.concatenate([by_source, by_target], axis=1)
    ng_ref[...] = (base_s[...] + mm_rt2(spread, w4)).astype(BF16)
    for p in range(3, 7):
        share(p)

    whole(bias_l, bs_send, bs_recv).wait_recv()
    bias = lax.fori_loop(1, n, lambda i, total: total + bias_l[i - 1], bias_s[...])
    gbi_ref[...] = bias[0:1, :] * edge_scale
    gbo_ref[...] = bias[1:2, :] * edge_scale
    gbn_ref[...] = bias[2:3, :] * node_scale
    gbq_ref[...] = bias[3:4, :] * node_scale
    whole(bias_l, bs_send, bs_recv).wait_send()
    whole(in1, px_send.at[0], px_recv.at[0, 0]).wait_send()
    whole(in2, px_send.at[1], px_recv.at[1, 0]).wait_send()
    whole(qlands, qs_send, qs_recv.at[0]).wait_send()
    whole(clands, cs_send, cs_recv.at[0]).wait_send()
    whole(qlands, gs_send, gs_recv).wait()


def deliver(*refs):
    count = len(refs) // 2
    sems = refs[-1]
    copies = [
        pltpu.make_async_copy(refs[i], refs[count + i], sems.at[i]) for i in range(count)
    ]
    for copy in copies:
        copy.start()
    for copy in copies:
        copy.wait()


_axis_order = ("dom", "rep")


def body(
    node_features, edge_features, node_cotangent, edge_cotangent,
    edge_in_weight, edge_in_bias, edge_out_weight, edge_out_bias,
    node_in_weight, node_in_bias, node_out_weight,
    edge_ends, live_elements, shared_nodes, shared_counts, multiplicity,
):
    n = lax.axis_size("dom")
    nodes, d = node_features.shape
    rows = edge_features.shape[0]
    edges = edge_ends.shape[1]
    s_count = shared_nodes.shape[2]
    hid = edge_in_weight.shape[1]
    edge_scale = 1.0 / math.sqrt(rows * n)
    node_scale = 1.0 / math.sqrt(nodes * n)
    slots = nodes // NPE
    quart = d // 4
    teams = n // 4
    vmem = pl.BlockSpec(memory_space=pltpu.VMEM)
    raw = pl.BlockSpec(memory_space=pl.ANY)
    hbm = pl.BlockSpec(memory_space=pltpu.HBM)
    shape = jax.ShapeDtypeStruct
    dma = pltpu.SemaphoreType.DMA
    vshape = pltpu.VMEM
    row = vshape((1, d), F32)
    args = (
        node_features, edge_features, node_cotangent, edge_cotangent,
        edge_in_weight, edge_in_bias.reshape(1, -1), edge_out_weight, edge_out_bias.reshape(1, -1),
        node_in_weight, node_in_bias.reshape(1, -1), node_out_weight,
        edge_ends, live_elements, shared_nodes[0], shared_counts,
        multiplicity.reshape(-1, LANES),
    )

    outs = pl.pallas_call(
        functools.partial(fused, n, n // 4, edge_scale, node_scale),
        out_shape=(
            vshape((nodes, d), BF16), vshape((rows, d), BF16),
            vshape((3 * d, hid), F32), row, vshape((hid, d), F32), row,
            vshape((2 * d, hid), F32), row, vshape((hid, d), F32), row,
        ),
        in_specs=[hbm] * 12 + [pl.BlockSpec(memory_space=pltpu.SMEM)] + [hbm] * 3,
        out_specs=(vmem,) * 10,
        scratch_shapes=[
            pltpu.VMEM((edges, LANES), F32), pltpu.VMEM((edges, LANES), F32),
            pltpu.VMEM((4 * s_count, LANES), F32), pltpu.VMEM((4, 8, s_count), F32),
            pltpu.VMEM((NPE, d), F32),
            pltpu.VMEM((edges, slots * d), BF16), pltpu.VMEM((edges, slots * d), BF16),
            pltpu.VMEM((edges, slots * hid), BF16), pltpu.VMEM((edges, slots * hid), F32),
            pltpu.VMEM((edges, slots * hid), F32), pltpu.VMEM((edges, slots * d), BF16),
            pltpu.VMEM((3 * slots * d, edges), BF16), pltpu.VMEM((edges, slots * hid), BF16),
            pltpu.VMEM((NPE, slots * hid), F32), pltpu.VMEM((2 * hid, nodes), BF16),
            pltpu.VMEM((2 * hid, 4 * s_count), BF16), pltpu.VMEM((hid, d), F32),
            pltpu.VMEM((nodes, d), BF16), pltpu.VMEM((NPE, slots * hid), F32),
            pltpu.VMEM((NPE, slots * hid), F32), pltpu.VMEM((nodes, d), F32),
            pltpu.VMEM((nodes, d), F32), pltpu.VMEM((nodes, d), F32),
        ]
        + [pltpu.VMEM((4, s_count, d), F32)] * 4
        + [pltpu.VMEM(arg.shape, arg.dtype) for i, arg in enumerate(args) if i != 12]
        + [dma((len(args) - 1,))]
        + [pltpu.VMEM((4, d), F32), pltpu.VMEM((n - 1, 4, d), F32)]
        + [dma((2,)), dma((2, 4)), dma, dma]
        + [
            pltpu.VMEM((7, 4, quart, d), F32), pltpu.VMEM((7, 3, quart, d), F32),
            pltpu.VMEM((7, quart, d), F32), pltpu.VMEM((7, teams - 1, quart, d), F32),
        ]
        + [dma, dma((7,)), dma, dma((7,)), dma, dma],
        compiler_params=pltpu.CompilerParams(
            collective_id=0, has_side_effects=True, vmem_limit_bytes=60 << 20
        ),
    )(*args)
    outs = pl.pallas_call(
        deliver,
        out_shape=tuple(shape(out.shape, out.dtype) for out in outs),
        in_specs=[vmem] * len(outs),
        out_specs=(raw,) * len(outs),
        scratch_shapes=[dma((len(outs),))],
        compiler_params=pltpu.CompilerParams(vmem_limit_bytes=8 << 20),
    )(*outs)
    flat = lambda v: v.reshape(-1)
    return (
        outs[0], outs[1], outs[2], flat(outs[3]), outs[4], flat(outs[5]),
        outs[6], flat(outs[7]), outs[8], flat(outs[9]),
    )


def solution(mesh):
    global _axis_order
    _axis_order = tuple(mesh.axis_names)
    both = P(("rep", "dom"))
    both2 = P(("rep", "dom"), None)
    in_specs = (
        (both2,) * 4 + (P(),) * 8 + (both, P(("rep", "dom"), None, None), both2, both)
    )
    out_specs = (both2, both2) + (P("rep", None), P("rep")) * 4
    return jax.shard_map(body, mesh=mesh, in_specs=in_specs, out_specs=out_specs, check_vma=False)
```

```python
import functools
import math

import jax
import jax.numpy as jnp
from jax import lax
from jax.experimental import pallas as pl
from jax.experimental.pallas import tpu as pltpu
from jax.sharding import PartitionSpec as P

NPE = 512
LANES = 128
F32 = jnp.float32
BF16 = jnp.bfloat16
MESH = pl.DeviceIdType.MESH
CHUNK = 448


def divisor_up_to(total, cap):
    best = 16
    for size in range(16, cap + 1, 16):
        if total % size == 0:
            best = size
    return best


def mm(left, right):
    return lax.dot_general(left, right, (((1,), (0,)), ((), ())), preferred_element_type=F32)


def half_of(rows):
    return rows // 32 * 16


def in_two(step, left, right):
    cut = half_of(left.shape[0])
    return jnp.concatenate([step(left[:cut, :], right), step(left[cut:, :], right)], axis=0)


def mm2(left, right):
    return in_two(mm, left, right)


def mm_rt2(left, right):
    return in_two(mm_rt, left, right)


def mm_lt2(left, right):
    cut = half_of(left.shape[0])
    return mm_lt(left[:cut, :], right[:cut, :]) + mm_lt(left[cut:, :], right[cut:, :])


def mm_rt(left, right):
    return lax.dot_general(left, right, (((1,), (1,)), ((), ())), preferred_element_type=F32)


def mm_lt(left, right):
    return lax.dot_general(left, right, (((0,), (0,)), ((), ())), preferred_element_type=F32)


def halves(value):
    high = value.astype(BF16)
    low = (value - high.astype(F32)).astype(BF16)
    return high, low


def columns_of(row):
    return jnp.transpose(jnp.broadcast_to(row, (LANES, row.shape[1])))


def hits(ids, width, shift=0):
    lane = lax.broadcasted_iota(jnp.int32, ids.shape, 1).astype(F32)
    moved = ids + float(shift) if shift else ids
    tiles = [
        jnp.where(moved == lane + float(LANES * t + shift), 1.0, 0.0).astype(BF16)
        for t in range(width // LANES)
    ]
    return jnp.concatenate(tiles, axis=1)


def row_hits(row, height, shift=0):
    node = (lax.broadcasted_iota(jnp.int32, (height, row.shape[1]), 0) + shift).astype(F32)
    return jnp.where(row + float(shift) == node, 1.0, 0.0).astype(BF16)


def repeated(weight, times):
    rows, cols = weight.shape
    zero = jnp.zeros((rows, cols), weight.dtype)
    return jnp.concatenate(
        [
            jnp.concatenate([weight if a == b else zero for b in range(times)], axis=1)
            for a in range(times)
        ],
        axis=0,
    )


def activation(linear):
    squashed = 0.5 * jnp.tanh(0.5 * linear) + 0.5
    return linear * squashed, squashed * (1.0 + linear * (1.0 - squashed))


def fused(
    n, quarter, edge_scale, node_scale,
    nf_any, ef_any, nc_any, ec_any, wi_any, bi_any, wo_any, bo_any, wn_any, bn_any, wq_any,
    ends_any, live_any, lists_any, counts_any, mult_any,
    ng_ref, eg_ref, gwi_ref, gbi_ref, gwo_ref, gbo_ref, gwn_ref, gbn_ref, gwq_ref, gbq_ref,
    col_s, col_t, lcol, rows_s, deg_s, src_s, tgt_s, hid_s, slope_s, lin_s, giv_s, join_t, eb_s,
    sum_s, sum_t, pick_t, gwo_s, cot_s, hback_s, early_s, base_s, inv_s, agg_s,
    out1, in1, out2, in2,
    nf_ref, ef_ref, nc_ref, ec_ref, wi_ref, bi_ref, wo_ref, bo_ref, wn_ref, bn_ref, wq_ref,
    ends_ref, lists_ref, counts_ref, mult_ref, in_sem, bias_s, bias_l,
    px_send, px_recv, bs_send, bs_recv,
    qparts, qlands, mids, clands, qs_send, qs_recv, cs_send, cs_recv, gs_send, gs_recv,
):
    nodes = nf_ref.shape[0]
    d = nf_ref.shape[1]
    slots = nodes // NPE
    wide = slots * d
    edges = ends_ref.shape[1]
    me = lax.axis_index("dom")
    rep = lax.axis_index("rep")
    offsets = (1, -1, quarter, -quarter)
    order = _axis_order
    ch = divisor_up_to(edges, CHUNK)
    n_ch = edges // ch

    def device(index):
        return tuple(index if name == "dom" else rep for name in order)

    team, seat = me // 4, lax.rem(me, 4)
    teams = n // 4
    groups = (
        ((ends_any, ends_ref),),
        ((nf_any, nf_ref), (wi_any, wi_ref), (bi_any, bi_ref), (ef_any, ef_ref)),
        ((lists_any, lists_ref), (counts_any, counts_ref)),
        ((wo_any, wo_ref), (bo_any, bo_ref)),
        (
            (mult_any, mult_ref), (wq_any, wq_ref), (wn_any, wn_ref), (bn_any, bn_ref),
            (nc_any, nc_ref), (ec_any, ec_ref),
        ),
    )
    loads = []
    count = 0
    for group in groups:
        loads.append([])
        for source, target in group:
            loads[-1].append(pltpu.make_async_copy(source, target, in_sem.at[count]))
            loads[-1][-1].start()
            count += 1

    def arrive(which):
        for load in loads[which]:
            load.wait()

    barrier = pltpu.get_barrier_semaphore()

    def greet(i, carry):
        pl.semaphore_signal(
            barrier, inc=1, device_id=device(lax.rem(me + i, n)), device_id_type=MESH
        )
        return carry

    lax.fori_loop(1, n, greet, 0)

    arrive(0)
    ends = ends_ref[...].astype(F32)
    source_row, target_row = ends[0:1, :], ends[1:2, :]
    for start in range(0, edges, LANES):
        stop = min(start + LANES, edges)
        col_t[start:stop, :] = columns_of(ends[1:2, start:stop])
        col_s[start:stop, :] = columns_of(ends[0:1, start:stop])
    arrive(1)
    wi = wi_ref[...]
    ws, wt, we = wi[:d, :], wi[d : 2 * d, :], wi[2 * d :, :]
    by_slot = lambda v: jnp.concatenate(
        [v[e * NPE : (e + 1) * NPE, :] for e in range(slots)], axis=1
    )
    by_row = lambda v: jnp.concatenate(
        [v[:, e * d : (e + 1) * d] for e in range(slots)], axis=0
    )
    fold = lambda v: v[:, :d] + v[:, d:]
    pair_of = lambda v: jnp.concatenate(halves(v), axis=1)
    across = lambda ref, first, count, step: jnp.concatenate(
        [ref[e * step + first : e * step + first + count, :] for e in range(slots)], axis=1
    )
    twice = lambda v: jnp.concatenate([v] * slots, axis=1)
    nf2 = by_slot(nf_ref[...])
    w_in = jnp.concatenate([repeated(w, slots) for w in (ws, wt, we)], axis=0)
    bi_wide = twice(bi_ref[...])

    fwd = divisor_up_to(edges, 672)
    n_fwd = edges // fwd
    for c in range(n_fwd):
        rows = slice(c * fwd, (c + 1) * fwd)
        target = mm(hits(col_t[rows, :], NPE), nf2).astype(BF16)
        source = mm(hits(col_s[rows, :], NPE), nf2).astype(BF16)
        src_s[rows, :] = source
        tgt_s[rows, :] = target
        joined = jnp.concatenate([source, target, across(ef_ref, c * fwd, fwd, edges)], axis=1)
        hidden, slope = activation(mm2(joined, w_in) + bi_wide)
        hid_s[rows, :] = hidden.astype(BF16)
        slope_s[rows, :] = slope

    arrive(2)
    s_count = lists_ref.shape[1]
    lane_row = lax.broadcasted_iota(jnp.int32, (1, s_count), 1)
    for k in range(4):
        row = jnp.where(
            lane_row < counts_ref[:, k : k + 1], lists_ref[k : k + 1, :], -1
        ).astype(F32)
        rows_s[k] = jnp.broadcast_to(row, (8, s_count))
        lcol[k * s_count : (k + 1) * s_count, :] = columns_of(row)
    arrive(3)
    wo = wo_ref[...]
    wo_wide = repeated(wo, slots)
    nb = 128
    for b in range(NPE // nb):
        node_id = (lax.broadcasted_iota(jnp.int32, (nb, edges), 0) + b * nb).astype(F32)
        deg_s[b * nb : (b + 1) * nb, :] = jnp.broadcast_to(
            jnp.sum(jnp.where(target_row == node_id, 1.0, 0.0), axis=1, keepdims=True), (nb, d)
        )
    sums = mm(
        row_hits(target_row, NPE),
        jnp.concatenate([across(ef_ref, 0, edges, edges), hid_s[...]], axis=1),
    )
    sum_s[...] = sums[:, wide:]
    agg2 = (
        sums[:, :wide]
        + mm2(pair_of(sums[:, wide:]), jnp.concatenate([wo_wide, wo_wide], axis=0))
        + twice(deg_s[...] * bo_ref[...])
    )
    agg_s[...] = by_row(agg2)

    upper = me >= n // 2
    turns = [jnp.where(upper, a, b) for a, b in ((2, 3), (0, 1), (3, 2), (1, 0))]
    steps = [jnp.where(upper, offsets[a], offsets[b]) for a, b in ((2, 3), (0, 1), (3, 2), (1, 0))]

    def partner_copy(out, incoming, which, j):
        k = turns[j]
        other = k + 1 - 2 * lax.rem(k, 2)
        return pltpu.make_async_remote_copy(
            src_ref=out.at[k],
            dst_ref=incoming.at[other],
            send_sem=px_send.at[which],
            recv_sem=px_recv.at[which, other],
            device_id=device(lax.rem(me + steps[j] + n, n)),
            device_id_type=MESH,
        )

    def landing(out, incoming, which, j):
        k = turns[j]
        return pltpu.make_async_remote_copy(
            src_ref=out.at[k],
            dst_ref=incoming.at[k],
            send_sem=px_send.at[which],
            recv_sem=px_recv.at[which, k],
            device_id=device(lax.rem(me + 1, n)),
            device_id_type=MESH,
        )

    def send_shared(values, out, incoming, which):
        pair = pair_of(values)
        for k in range(4):
            out[k] = fold(
                mm(hits(lcol[k * s_count : (k + 1) * s_count, :], nodes, which), pair)
            )
        for j in ((1, 0, 3, 2), (0, 1, 3, 2))[which]:
            partner_copy(out, incoming, which, j).start()

    def landed(out, incoming, which, js):
        for j in js:
            landing(out, incoming, which, j).wait_recv()
        moved = jnp.concatenate([incoming[turns[j]] for j in js], axis=0)
        entries = jnp.concatenate([rows_s[turns[j]][0:1, :] for j in js], axis=1)
        return pair_of(moved), entries

    near, far = (2, 3), (0, 1)
    pl.semaphore_wait(barrier, n - 1)
    send_shared(agg_s[...], out1, in1, 0)

    arrive(4)
    mult = mult_ref[...].astype(F32)
    for b in range(nodes // LANES):
        inv_s[b * LANES : (b + 1) * LANES, :] = 1.0 / columns_of(mult[b : b + 1, :])
    live = live_any[0]
    slot_of = lax.broadcasted_iota(jnp.int32, (nodes, d), 0) // NPE
    node_cot = jnp.where(slot_of < live, nc_ref[...].astype(F32), 0.0)
    cot_s[...] = node_cot.astype(BF16)
    wn = wn_ref[...]
    wn_wide = repeated(wn[d:, :], slots)
    hback_s[...] = mm_rt2(by_slot(cot_s[...]), repeated(wq_ref[...], slots))
    early_s[...] = mm2(nf2, repeated(wn[:d, :], slots)) + twice(bn_ref[...])
    bias_s[...] = jnp.zeros_like(bias_s)
    bias_s[3:4, :] = jnp.sum(node_cot, axis=0, keepdims=True)

    given_sum = jnp.zeros((1, d), F32)
    gwo = jnp.zeros((d, d), F32)
    for e in range(slots):
        lanes = slice(e * d, (e + 1) * d)
        given = jnp.where(
            jnp.broadcast_to(live, (edges, d)) > e,
            ec_ref[e * edges : (e + 1) * edges, :].astype(F32),
            0.0,
        )
        given_sum = given_sum + jnp.sum(given, axis=0, keepdims=True)
        giv_s[:, lanes] = given.astype(BF16)
        gwo = gwo + mm_lt(hid_s[:, lanes], giv_s[:, lanes])
    gwo_s[...] = gwo
    lin_s[...] = mm_rt2(giv_s[...], wo_wide)
    for at, block in enumerate((src_s[...], tgt_s[...], across(ef_ref, 0, edges, edges))):
        join_t[at * wide : (at + 1) * wide, :] = jnp.transpose(block)
    sum_rows = pair_of(by_row(sum_s[...]))
    picked = fold(mm2(hits(lcol[...], nodes, 2), sum_rows))
    pick_t[...] = jnp.transpose(pair_of(picked))
    sum_t[...] = jnp.transpose(sum_rows)

    def gather_in(js):
        moved, entries = landed(out1, in1, 0, js)
        return agg_s[...] + fold(mm2(row_hits(entries, nodes), moved))

    agg_s[...] = gather_in(near)
    consistent = (gather_in(far) * inv_s[...]).astype(BF16)
    node_hidden, node_slope = activation(early_s[...] + mm2(by_slot(consistent), wn_wide))
    node_back2 = (hback_s[...] * node_slope).astype(BF16)
    back = by_row(mm_rt2(node_back2, wn_wide)) * inv_s[...]
    agg_s[...] = back
    send_shared(back, out2, in2, 1)

    quart = qparts.shape[2]
    results = (
        (gwn_ref, 0, node_scale), (gwn_ref, d, node_scale), (gwq_ref, 0, node_scale),
        (gwo_ref, 0, edge_scale),
        (gwi_ref, 2 * d, edge_scale), (gwi_ref, d, edge_scale), (gwi_ref, 0, edge_scale),
    )

    def seat_of(i):
        if i == 1:
            return seat + 1 - 2 * lax.rem(seat, 2)
        return lax.rem(seat + 2, 4) if i == 2 else 3 - seat

    def split_copy(p, i):
        return pltpu.make_async_remote_copy(
            src_ref=qparts.at[p, seat_of(i)],
            dst_ref=qlands.at[p, i - 1],
            send_sem=qs_send,
            recv_sem=qs_recv.at[p],
            device_id=device(4 * team + seat_of(i)),
            device_id_type=MESH,
        )

    def cross_copy(p, i):
        return pltpu.make_async_remote_copy(
            src_ref=mids.at[p],
            dst_ref=clands.at[p, i - 1],
            send_sem=cs_send,
            recv_sem=cs_recv.at[p],
            device_id=device(4 * lax.rem(team + i, teams) + seat),
            device_id_type=MESH,
        )

    def share_copy(p, i):
        ref, first, _ = results[p]
        rows = pl.ds(pl.multiple_of(first + seat * quart, 8), quart)
        return pltpu.make_async_remote_copy(
            src_ref=ref.at[rows],
            dst_ref=ref.at[rows],
            send_sem=gs_send,
            recv_sem=gs_recv,
            device_id=device(4 * team + seat_of(i)),
            device_id_type=MESH,
        )

    def whole(ref, send_sem, recv_sem):
        return pltpu.make_async_remote_copy(
            src_ref=ref,
            dst_ref=ref,
            send_sem=send_sem,
            recv_sem=recv_sem,
            device_id=device(lax.rem(me + 1, n)),
            device_id_type=MESH,
        )

    def hold(p, value):
        for j in range(4):
            qparts[p, j] = value[j * quart : (j + 1) * quart, :]

    def push(p):
        for i in (3, 2, 1):
            split_copy(p, i).start()

    def cross(p):
        whole(qlands.at[p], qs_send, qs_recv.at[p]).wait_recv()
        total = qparts[p, seat]
        for i in range(3):
            total = total + qlands[p, i]
        mids[p] = total
        for i in range(1, teams):
            cross_copy(p, i).start()

    def share(p):
        whole(clands.at[p], cs_send, cs_recv.at[p]).wait_recv()
        total = mids[p]
        for i in range(teams - 1):
            total = total + clands[p, i]
        ref, first, scale = results[p]
        ref[pl.ds(pl.multiple_of(first + seat * quart, 8), quart), :] = total * scale
        for i in (3, 2, 1):
            share_copy(p, i).start()

    node_back = by_row(node_back2)
    hold(0, mm_lt2(nf_ref[...], node_back))
    hold(1, mm_lt2(consistent, node_back))
    hold(2, mm_lt2(by_row(node_hidden.astype(BF16)), cot_s[...]))
    for p in range(3):
        push(p)
    bias_s[2:3, :] = jnp.sum(node_back.astype(F32), axis=0, keepdims=True)
    base_s[...] = cot_s[...].astype(F32) + mm_rt2(node_back, wn[:d, :])
    wo_rows = jnp.concatenate([wo, wo], axis=1)
    pair_back = pair_of(back)
    crossed = mm2(sum_t[...], pair_back)
    gwo_s[...] = gwo_s[...] + fold(crossed[:d, :]) + fold(crossed[d:, :])
    spread_back = by_slot(mm_rt2(pair_back, wo_rows))
    for c in range(n_ch):
        rows = slice(c * ch, (c + 1) * ch)
        got = mm(hits(col_t[rows, :], NPE, 1), pair_of(spread_back))
        lin_s[rows, :] = lin_s[rows, :] + got[:, :wide] + got[:, wide:]

    def toward(moved, entries, e):
        wanted = entries - float(NPE * e)
        marks = jnp.concatenate(
            [
                jnp.where(col_t[...] == wanted[:, t * LANES : (t + 1) * LANES], 1.0, 0.0).astype(BF16)
                for t in range(entries.shape[1] // LANES)
            ],
            axis=1,
        )
        return fold(mm2(marks, moved))

    moved, entries = landed(out2, in2, 1, near)
    moved = pair_of(mm_rt2(moved, wo_rows))
    for e in range(slots):
        lanes = slice(e * d, (e + 1) * d)
        lin_s[:, lanes] = lin_s[:, lanes] + toward(moved, entries, e)
    moved, entries = landed(out2, in2, 1, far)
    moved = pair_of(mm_rt2(moved, wo_rows))
    for e in range(slots):
        lanes = slice(e * d, (e + 1) * d)
        eb_s[:, lanes] = (
            (lin_s[:, lanes] + toward(moved, entries, e)) * slope_s[:, lanes]
        ).astype(BF16)
    arrived = pair_of(jnp.concatenate([in2[k] for k in range(4)], axis=0))
    added = mm2(pick_t[...], arrived)
    hold(3, gwo_s[...] + fold(added[:d, :]) + fold(added[d:, :]))
    push(3)

    def weigh(at):
        total = None
        for e in range(slots):
            first = at * wide + e * d
            both = mm(join_t[first : first + d, :], eb_s[...])[:, e * d : (e + 1) * d]
            total = both if total is None else total + both
        return total

    for at in (2, 1, 0):
        hold(6 - at, weigh(at))
        push(6 - at)
    for p in range(0, 3):
        cross(p)
    column = jnp.sum(eb_s[...].astype(F32), axis=0, keepdims=True)
    bias_row = column[:, :d]
    for e in range(1, slots):
        bias_row = bias_row + column[:, e * d : (e + 1) * d]
    bias_s[0:1, :] = bias_row
    entry_row = jnp.concatenate([rows_s[k][0:1, :] for k in range(4)], axis=1)
    agg_back = agg_s[...] + fold(mm2(row_hits(entry_row, nodes, 1), arrived))
    degrees = jnp.concatenate([deg_s[...]] * slots, axis=0)
    bias_s[1:2, :] = given_sum + jnp.sum(degrees * agg_back, axis=0, keepdims=True)

    def bias_copy(i):
        return pltpu.make_async_remote_copy(
            src_ref=bias_s,
            dst_ref=bias_l.at[i - 1],
            send_sem=bs_send,
            recv_sem=bs_recv,
            device_id=device(lax.rem(me + i, n)),
            device_id_type=MESH,
        )

    eb2 = eb_s[...]
    we_wide = repeated(we, slots)
    quad = pair_of(by_slot(agg_back))
    for c in range(n_ch):
        rows = slice(c * ch, (c + 1) * ch)
        got = mm(hits(col_t[rows, :], NPE, 2), quad)
        cot = giv_s[rows, :].astype(F32) + (got[:, :wide] + got[:, wide:])
        value = (cot + mm_rt(eb_s[rows, :], we_wide)).astype(BF16)
        for e in range(slots):
            eg_ref[e * edges + c * ch : e * edges + (c + 1) * ch, :] = value[
                :, e * d : (e + 1) * d
            ]
    cross(3)
    lax.fori_loop(1, n, lambda i, x: (bias_copy(i).start(), x)[1], 0)

    by_target = pair_of(by_row(mm2(row_hits(target_row, NPE, 1), eb2)))
    for p in range(4, 7):
        cross(p)
    for p in range(0, 3):
        share(p)
    by_source = pair_of(by_row(mm2(row_hits(source_row, NPE, 1), eb2)))
    w4 = jnp.concatenate([ws, ws, wt, wt], axis=1)
    spread = jnp.concatenate([by_source, by_target], axis=1)
    ng_ref[...] = (base_s[...] + mm_rt2(spread, w4)).astype(BF16)
    for p in range(3, 7):
        share(p)

    whole(bias_l, bs_send, bs_recv).wait_recv()
    bias = lax.fori_loop(1, n, lambda i, total: total + bias_l[i - 1], bias_s[...])
    gbi_ref[...] = bias[0:1, :] * edge_scale
    gbo_ref[...] = bias[1:2, :] * edge_scale
    gbn_ref[...] = bias[2:3, :] * node_scale
    gbq_ref[...] = bias[3:4, :] * node_scale
    whole(bias_l, bs_send, bs_recv).wait_send()
    whole(in1, px_send.at[0], px_recv.at[0, 0]).wait_send()
    whole(in2, px_send.at[1], px_recv.at[1, 0]).wait_send()
    whole(qlands, qs_send, qs_recv.at[0]).wait_send()
    whole(clands, cs_send, cs_recv.at[0]).wait_send()
    whole(qlands, gs_send, gs_recv).wait()


def deliver(*refs):
    count = len(refs) // 2
    sems = refs[-1]
    copies = [
        pltpu.make_async_copy(refs[i], refs[count + i], sems.at[i]) for i in range(count)
    ]
    for copy in copies:
        copy.start()
    for copy in copies:
        copy.wait()


_axis_order = ("dom", "rep")


def body(
    node_features, edge_features, node_cotangent, edge_cotangent,
    edge_in_weight, edge_in_bias, edge_out_weight, edge_out_bias,
    node_in_weight, node_in_bias, node_out_weight,
    edge_ends, live_elements, shared_nodes, shared_counts, multiplicity,
):
    n = lax.axis_size("dom")
    nodes, d = node_features.shape
    rows = edge_features.shape[0]
    edges = edge_ends.shape[1]
    s_count = shared_nodes.shape[2]
    hid = edge_in_weight.shape[1]
    edge_scale = 1.0 / math.sqrt(rows * n)
    node_scale = 1.0 / math.sqrt(nodes * n)
    slots = nodes // NPE
    quart = d // 4
    teams = n // 4
    vmem = pl.BlockSpec(memory_space=pltpu.VMEM)
    raw = pl.BlockSpec(memory_space=pl.ANY)
    hbm = pl.BlockSpec(memory_space=pltpu.HBM)
    shape = jax.ShapeDtypeStruct
    dma = pltpu.SemaphoreType.DMA
    vshape = pltpu.VMEM
    row = vshape((1, d), F32)
    args = (
        node_features, edge_features, node_cotangent, edge_cotangent,
        edge_in_weight, edge_in_bias.reshape(1, -1), edge_out_weight, edge_out_bias.reshape(1, -1),
        node_in_weight, node_in_bias.reshape(1, -1), node_out_weight,
        edge_ends, live_elements, shared_nodes[0], shared_counts,
        multiplicity.reshape(-1, LANES),
    )

    outs = pl.pallas_call(
        functools.partial(fused, n, n // 4, edge_scale, node_scale),
        out_shape=(
            vshape((nodes, d), BF16), vshape((rows, d), BF16),
            vshape((3 * d, hid), F32), row, vshape((hid, d), F32), row,
            vshape((2 * d, hid), F32), row, vshape((hid, d), F32), row,
        ),
        in_specs=[hbm] * 12 + [pl.BlockSpec(memory_space=pltpu.SMEM)] + [hbm] * 3,
        out_specs=(vmem,) * 10,
        scratch_shapes=[
            pltpu.VMEM((edges, LANES), F32), pltpu.VMEM((edges, LANES), F32),
            pltpu.VMEM((4 * s_count, LANES), F32), pltpu.VMEM((4, 8, s_count), F32),
            pltpu.VMEM((NPE, d), F32),
            pltpu.VMEM((edges, slots * d), BF16), pltpu.VMEM((edges, slots * d), BF16),
            pltpu.VMEM((edges, slots * hid), BF16), pltpu.VMEM((edges, slots * hid), F32),
            pltpu.VMEM((edges, slots * hid), F32), pltpu.VMEM((edges, slots * d), BF16),
            pltpu.VMEM((3 * slots * d, edges), BF16), pltpu.VMEM((edges, slots * hid), BF16),
            pltpu.VMEM((NPE, slots * hid), F32), pltpu.VMEM((2 * hid, nodes), BF16),
            pltpu.VMEM((2 * hid, 4 * s_count), BF16), pltpu.VMEM((hid, d), F32),
            pltpu.VMEM((nodes, d), BF16), pltpu.VMEM((NPE, slots * hid), F32),
            pltpu.VMEM((NPE, slots * hid), F32), pltpu.VMEM((nodes, d), F32),
            pltpu.VMEM((nodes, d), F32), pltpu.VMEM((nodes, d), F32),
        ]
        + [pltpu.VMEM((4, s_count, d), F32)] * 4
        + [pltpu.VMEM(arg.shape, arg.dtype) for i, arg in enumerate(args) if i != 12]
        + [dma((len(args) - 1,))]
        + [pltpu.VMEM((4, d), F32), pltpu.VMEM((n - 1, 4, d), F32)]
        + [dma((2,)), dma((2, 4)), dma, dma]
        + [
            pltpu.VMEM((7, 4, quart, d), F32), pltpu.VMEM((7, 3, quart, d), F32),
            pltpu.VMEM((7, quart, d), F32), pltpu.VMEM((7, teams - 1, quart, d), F32),
        ]
        + [dma, dma((7,)), dma, dma((7,)), dma, dma],
        compiler_params=pltpu.CompilerParams(
            collective_id=0, has_side_effects=True, vmem_limit_bytes=60 << 20
        ),
    )(*args)
    outs = pl.pallas_call(
        deliver,
        out_shape=tuple(shape(out.shape, out.dtype) for out in outs),
        in_specs=[vmem] * len(outs),
        out_specs=(raw,) * len(outs),
        scratch_shapes=[dma((len(outs),))],
        compiler_params=pltpu.CompilerParams(vmem_limit_bytes=8 << 20),
    )(*outs)
    flat = lambda v: v.reshape(-1)
    return (
        outs[0], outs[1], outs[2], flat(outs[3]), outs[4], flat(outs[5]),
        outs[6], flat(outs[7]), outs[8], flat(outs[9]),
    )


def solution(mesh):
    global _axis_order
    _axis_order = tuple(mesh.axis_names)
    both = P(("rep", "dom"))
    both2 = P(("rep", "dom"), None)
    in_specs = (
        (both2,) * 4 + (P(),) * 8 + (both, P(("rep", "dom"), None, None), both2, both)
    )
    out_specs = (both2, both2) + (P("rep", None), P("rep")) * 4
    return jax.shard_map(body, mesh=mesh, in_specs=in_specs, out_specs=out_specs, check_vma=False)
```
